32 devices in a mesh: groups: 2 (over x), tm: 16 (over z, y, core).
Axes of the slice: x: 2, y: 2, z: 4, core: 2. Of those that a mesh axis runs over, the one named last changes fastest.
Arguments:
- records: bfloat16 [384, 4096], P('groups', 'tm'), parts along dimension 0, may hold values from -6 to 6
- bank: bfloat16 [256, 384, 240], P('tm', 'groups'), parts along dimension 1, may hold values from -6 to 6
- plan: int32 [6], P('groups'), parts along dimension 0, may hold values from 0 to 15
- template_ids: int32 [6, 2], P('groups'), parts along dimension 0, may hold values from 0 to 15
- channel_mask: int32 [384], P('groups'), parts along dimension 0, may hold values 0 or 1
Outputs:
- detection: float32 [6, 2, 4096], P('groups', None, 'tm'), parts along dimension 0
The draws below stay inside these ranges and needn't reach their ends.
There are 2 independent parts, one for each index of `groups`. The reference program is written for one: setup_inputs(seed, part) draws one part's arguments, and reference() takes and returns one part's arrays. A program takes and returns all parts, laid end to end along the dimension named above; each array names one. Nothing has to cross between parts.
Inputs may be any that keep to these rules, and one draw needn't show every extreme that they name: `plan`: the index of tm that holds a step's templates. `template_ids`: slots within the owner's 16 templates.
All inputs are finite; a program needn't handle non-finite values.
Results may differ from the reference program's by a relative error of at most 0.0003.
Values may be sent and summed in bfloat16 or wider, within the bound.
A program may use at most 64 MiB of HBM per device.

```python
import jax
import jax.numpy as jnp
from jax import lax

C = 192
L = 240
K = 2
STEPS = 3
SLOTS = 16
TOTAL = 4096
BANK = 256
N_TM = 16


def place_ends(values, stream_key, low, largest):
    longest = values.shape.index(max(values.shape))
    spots = []
    for shift in (0, 1):
        where = [jax.random.randint(jax.random.fold_in(stream_key, axis), (), 0, length) for axis, length in enumerate(values.shape)]
        where[longest] = (where[longest] + shift) % values.shape[longest]
        spots.append(tuple(where))
    return values.at[spots[0]].set(low).at[spots[1]].set(largest)


def steps_of(stream_key, shape, cuts, least, high):
    def one(position, blocks):
        steps = jax.random.uniform(jax.random.fold_in(jax.random.fold_in(stream_key, 6), position), (blocks,), jnp.float32, least / len(cuts), high / len(cuts))
        return jnp.repeat(jnp.exp(steps), shape[position] // blocks).reshape((-1,) + (1,) * (len(shape) - position - 1))

    loudness = one(*cuts[0])
    for cut in cuts[1:]:
        loudness = loudness * one(*cut)
    return loudness


def noise(own_key, dims, width, reach, pieces=(), held_as=jnp.bfloat16):
    values = width * jax.random.normal(own_key, dims, jnp.float32)
    if pieces:
        values = values * steps_of(own_key, dims, pieces, -0.22, 0.18)
    return jnp.clip(values, -reach, reach).astype(held_as)


def setup_inputs(seed: int = 0, part: int = 0) -> dict:
    key_list = jax.random.split(jax.random.key(seed), 6)
    part_keys = jax.random.split(jax.random.fold_in(key_list[5], part), 6)
    return {
        "records": noise(part_keys[0], (C, TOTAL), 1.0, 6.0, ((1, 16),)),
        "bank": noise(part_keys[1], (BANK, C, L), 1.0, 6.0, ((0, 16),)),
        "plan": jax.random.randint(part_keys[2], (STEPS,), 0, N_TM).astype(jnp.int32),
        "template_ids": place_ends(jax.random.randint(part_keys[3], (STEPS, K), 0, SLOTS), jax.random.fold_in(part_keys[3], 1), 0, SLOTS - 1).astype(jnp.int32),
        "channel_mask": place_ends((jax.random.randint(part_keys[4], (C,), 0, 4) < 3).astype(jnp.int32), jax.random.fold_in(part_keys[4], 1), 0, 1),
    }


def correlate(extended, chosen, inv_norm, mask_f, scale):
    kcount, chans, taps = chosen.shape
    kernel = jnp.transpose(chosen, (1, 0, 2)).reshape(chans * kcount, 1, taps)
    raw = lax.conv_general_dilated(extended[None], kernel, (1,), 'VALID', dimension_numbers=('NCH', 'OIH', 'NCH'), feature_group_count=chans, preferred_element_type=jnp.float32)[0]
    raw = raw.reshape(chans, kcount, -1)
    chosen_f = chosen.astype(jnp.float32)
    weight = mask_f[None, :] / jnp.sqrt(lax.optimization_barrier(jnp.sum(chosen_f * chosen_f, axis=2)) + 1e-06)
    normed = raw * inv_norm[:, None, :]
    return scale * jnp.einsum('kc,ckt->kt', weight, normed, precision=lax.Precision.HIGHEST)

def reference(records, bank, plan, template_ids, channel_mask):
    taps = bank.shape[2]
    chans = records.shape[0]
    extended = jnp.concatenate([records, jnp.zeros((chans, taps - 1), records.dtype)], axis=1)
    sq = extended.astype(jnp.float32) ** 2
    energy = lax.reduce_window(sq, jnp.array(0.0, sq.dtype), lax.add, (1, taps), (1, 1), 'VALID')
    inv_norm = 1.0 / jnp.sqrt(energy + 1e-06)
    mask_f = channel_mask.astype(jnp.float32)
    scale = jnp.sqrt(taps / (1.0 + jnp.sum(mask_f)))

    def one_step(pair):
        owner, ids = pair
        rows = (owner * SLOTS + ids).astype(jnp.int32)
        chosen = jnp.take(bank, rows, axis=0)
        return correlate(extended, chosen, inv_norm, mask_f, scale)
    return lax.map(one_step, (plan, template_ids))
```

```python
import functools

import jax
import jax.numpy as jnp
from jax import lax
from jax.experimental import pallas as pl
from jax.experimental.pallas import tpu as pltpu
from jax.sharding import PartitionSpec as P

MESH = pl.DeviceIdType.MESH
LANES = 128


def up(value, unit):
    return -(-value // unit) * unit


def kernel(
    n, steps, kk, taps,
    plan_in, ids_in, mask_in, row_in, rec_ref, bank_ref, out_ref,
    plan_ref, ids_ref, mask_s, mask_v, bank_v, tsend, tpart, tcomb, trecv, rrecv, xs, frames, inv, tmpl, wts, acc, osend, orecv,
    ready, few_sem, bank_sem, rs_sem, rr_sem, fs_sem, fr_sem, cs_sem, cr_sem, ts_sem, tr_sem, os_sem, or_sem,
):
    me = lax.axis_index("tm")
    chip, core = me // 2, me % 2
    chips = n // 2
    partner = me + 1 - 2 * core
    chans, block = rec_ref.shape
    own = chans // chips
    halves = block // LANES
    part = LANES // 2
    width = frames.shape[2] // LANES
    dims = (((1,), (1,)), ((), ()))

    def tell(sem, to):
        pl.semaphore_signal(sem, inc=1, device_id={"tm": to}, device_id_type=MESH)

    def push(src, dst, send_sem, recv_sem, to):
        return pltpu.make_async_remote_copy(
            src_ref=src, dst_ref=dst, send_sem=send_sem, recv_sem=recv_sem,
            device_id={"tm": to}, device_id_type=MESH,
        )

    barrier = pltpu.get_barrier_semaphore()
    tell(barrier, partner)

    @pl.loop(chip + 1, chips)
    def _(q):
        tell(barrier, 2 * q)
        tell(barrier, 2 * q + 1)

    fetch = pltpu.make_async_copy(bank_ref, bank_v, bank_sem)
    fetch.start()
    few = [
        pltpu.make_async_copy(src, dst, few_sem.at[i])
        for i, (src, dst) in enumerate([(plan_in, plan_ref), (ids_in, ids_ref), (mask_in, mask_s), (row_in, mask_v)])
    ]
    for copy in few:
        copy.start()
    pl.semaphore_wait(barrier, 1 + 2 * chip)

    @pl.loop(0, chip)
    def _(q):
        tell(ready.at[chip], 2 * q)
        tell(ready.at[chip], 2 * q + 1)

    def send_records(q):
        rows = pl.ds(pl.multiple_of(q * own, 8), own)
        return push(rec_ref.at[rows], rrecv.at[core, chip], rs_sem, rr_sem, 2 * q + core)

    def across(s):
        return push(tsend.at[s], tpart.at[s], cs_sem.at[s], cr_sem.at[s], partner)

    def spread(s, q):
        return push(tcomb.at[s, q], trecv[s].at[chip], ts_sem, tr_sem.at[s], 2 * q + core)

    @pl.loop(0, chip)
    def _(q):
        send_records(q).start()

    keep = pltpu.make_async_copy(
        rec_ref.at[pl.ds(pl.multiple_of(chip * own, 8), own)], rrecv.at[core, chip], bank_sem
    )
    for copy in few:
        copy.wait()
    fetch.wait()
    keep.start()
    for s in range(steps):
        for j in range(kk):
            pick = bank_v[ids_ref[(1 - core) * kk + j, s]]
            for q in range(chips):
                tsend[s, q, j] = pick[q * own : (q + 1) * own]
        across(s).start()
    for s in range(steps):
        theirs = plan_ref[s] == partner
        across(s).wait_recv()
        for j in range(kk):
            pick = bank_v[ids_ref[core * kk + j, s]]
            for q in range(chips):
                tcomb[s, q, j] = jnp.where(theirs, tpart[s, q, j], pick[q * own : (q + 1) * own])
        trecv[s][chip] = tcomb[s, chip]

        @pl.loop(0, chip)
        def _(q):
            spread(s, q).start()

    @pl.loop(chip + 1, chips)
    def _(q):
        pl.semaphore_wait(ready.at[q], 2)
        send_records(q).start()
        spread(0, q).start()

    for s in range(1, steps):

        @pl.loop(chip + 1, chips)
        def _(q):
            spread(s, q).start()

    keep.wait()
    others = pl.ds(0, chips - 1)
    got_records = push(rrecv.at[0, others], rrecv.at[0, others], rs_sem, rr_sem, partner)
    got_records.wait_recv()
    forward = push(rrecv.at[core], rrecv.at[core], fs_sem, fr_sem, partner)
    forward.start()
    forward.wait_recv()

    for v in range(halves):
        for a in range(n):
            xs[v, a * own : (a + 1) * own, :] = rrecv[a % 2, a // 2, :, v * LANES : (v + 1) * LANES].astype(jnp.float32)
        xs[v, n * own :, :] = jnp.zeros((xs.shape[1] - n * own, LANES), jnp.float32)
    shift = lax.broadcasted_iota(jnp.int32, (part, width * LANES), 1) - lax.broadcasted_iota(
        jnp.int32, (part, width * LANES), 0
    )
    band = jnp.where((shift >= 0) & (shift < taps), 1.0, 0.0).astype(jnp.bfloat16)
    live = jnp.sum(mask_v[...].astype(jnp.float32), axis=1, keepdims=True)
    scale = jnp.sqrt(taps / (1.0 + live))
    left = lax.broadcasted_iota(jnp.int32, (n, LANES), 1) < part

    def frame(i, carry):
        tiles = [
            xs[q % halves, pl.ds(i + (q // halves) * own, n, stride=own), :] for q in range(halves + width)
        ]
        turned = [pltpu.roll(tile, part, 1) for tile in tiles]
        odd = [jnp.where(left, turned[q], turned[q + 1]) for q in range(halves + width - 1)]
        x = jnp.concatenate(
            [jnp.concatenate(some[h : h + width], axis=1) for some in (tiles, odd) for h in range(halves)], axis=0
        )
        frames[i] = x.astype(jnp.bfloat16)
        sq = x * x
        high = sq.astype(jnp.bfloat16)
        low = (sq - high.astype(jnp.float32)).astype(jnp.bfloat16)
        energy = lax.dot_general(
            jnp.concatenate([high, low], axis=0), band, dims, preferred_element_type=jnp.float32
        )
        energy = energy[: 2 * halves * n] + energy[2 * halves * n :]
        factor = scale * mask_s[chip * own + i].astype(jnp.float32)
        inv[i] = factor / jnp.sqrt(energy + 1e-06)
        return carry

    lax.fori_loop(0, own, frame, 0, unroll=own)

    for s in range(steps):
        some = trecv[s].at[others]
        push(some, some, ts_sem, tr_sem.at[s], partner).wait_recv()
        for j in range(kk):
            got = trecv[s][lax.div(plan_ref[s], 2), j].astype(jnp.float32)
            tmpl[...] = jnp.concatenate([got, jnp.zeros((own, width * LANES - taps), jnp.float32)], axis=1)
            energy = jnp.sum(got * got, axis=1, keepdims=True)
            wts[...] = jnp.broadcast_to(1.0 / jnp.sqrt(energy + 1e-06), (own, part))

            def channel(i, total):
                base = jnp.broadcast_to(tmpl[pl.ds(i, 1), :], (16, width * LANES)).astype(jnp.bfloat16)
                base = jnp.concatenate([base] * (part // 16), axis=0)
                taps_of = pltpu.roll(base, 0, 1, stride=1, stride_axis=0)
                raw = lax.dot_general(frames[i], taps_of, dims, preferred_element_type=jnp.float32)
                return total + raw * inv[i] * wts[pl.ds(i, 1), :]

            total = lax.fori_loop(0, own, channel, jnp.zeros((2 * halves * n, part), jnp.float32), unroll=own)
            total = jnp.concatenate([total[: halves * n], total[halves * n :]], axis=1)
            at = (s * kk + j) * halves * n
            acc[at : at + halves * n, :] = total

    rows = steps * kk * halves
    for d in range(n):
        osend[d] = acc[pl.ds(d, rows, stride=n), :]
    orecv[me] = osend[me]

    def give(d):
        return push(osend.at[d], orecv.at[me], os_sem, or_sem, d)

    @pl.loop(0, me)
    def _(d):
        give(d).start()

    @pl.loop(me + 1, n)
    def _(d):
        give(d).start()

    sums = orecv.at[pl.ds(0, n - 1)]
    push(sums, sums, os_sem, or_sem, partner).wait_recv()
    totals = jnp.sum(orecv[...].reshape(chips, 2, rows, LANES), axis=0)
    for c in range(2):
        final = totals[c]
        for s in range(steps):
            for j in range(kk):
                for h in range(halves):
                    r = (s * kk + j) * halves + h
                    out_ref[s, c * kk + j, h * LANES : (h + 1) * LANES] = final[r]

    got_records.wait_send()
    forward.wait_send()
    for s in range(steps):
        across(s).wait_send()
    some = tcomb.at[:, others]
    push(some, some, ts_sem, tr_sem.at[0], partner).wait_send()
    push(sums, sums, os_sem, or_sem, partner).wait_send()


def shards(records, bank, plan, template_ids, channel_mask):
    n = lax.axis_size("tm")
    chips = n // 2
    steps, kcount = template_ids.shape
    chans, block = records.shape
    slots, _, taps = bank.shape
    kk = kcount // 2
    own = up(chans // chips, 8)
    if own * chips != chans:
        few = chans // chips
        more = own - few
        records = jnp.pad(records.reshape(chips, few, block), ((0, 0), (0, more), (0, 0))).reshape(-1, block)
        bank = jnp.pad(bank.reshape(slots, chips, few, taps), ((0, 0), (0, 0), (0, more), (0, 0))).reshape(slots, -1, taps)
        channel_mask = jnp.pad(channel_mask.reshape(chips, few), ((0, 0), (0, more))).reshape(-1)
    halves = block // LANES
    part = LANES // 2
    width = up(part + taps - 1, LANES) // LANES
    vmem = pl.BlockSpec(memory_space=pltpu.VMEM)
    hbm = pl.BlockSpec(memory_space=pl.ANY)
    f32, bf16 = jnp.float32, jnp.bfloat16
    dma = pltpu.SemaphoreType.DMA
    extra = -(-(halves + width - 1) // halves)
    rows = steps * kk * halves
    return pl.pallas_call(
        functools.partial(kernel, n, steps, kk, taps),
        out_shape=jax.ShapeDtypeStruct((steps, kcount, block), f32),
        in_specs=[hbm] * 6,
        out_specs=vmem,
        scratch_shapes=[
            pltpu.SMEM((steps,), jnp.int32),
            pltpu.SMEM((kcount, steps), jnp.int32),
            pltpu.SMEM(channel_mask.shape, jnp.int32),
            pltpu.VMEM((1, channel_mask.shape[0]), jnp.int32),
            pltpu.VMEM(bank.shape, bf16),
            pltpu.VMEM((steps, chips, kk, own, taps), bf16),
            pltpu.VMEM((steps, chips, kk, own, taps), bf16),
            pltpu.VMEM((steps, chips, kk, own, taps), bf16),
            [pltpu.VMEM((chips, kk, own, taps), bf16)] * steps,
            pltpu.VMEM((2, chips, own, block), bf16),
            pltpu.VMEM((halves, (n + extra) * own, LANES), f32),
            pltpu.VMEM((own, 2 * halves * n, width * LANES), bf16),
            pltpu.VMEM((own, 2 * halves * n, part), f32),
            pltpu.VMEM((own, width * LANES), f32),
            pltpu.VMEM((own, part), f32),
            pltpu.VMEM((rows * n, LANES), f32),
            pltpu.VMEM((n, rows, LANES), f32),
            pltpu.VMEM((n, rows, LANES), f32),
            pltpu.SemaphoreType.REGULAR((chips,)),
            dma((4,)), dma(()), dma(()), dma(()), dma(()), dma(()), dma((steps,)), dma((steps,)), dma(()), dma((steps,)),
            dma(()), dma(()),
        ],
        compiler_params=pltpu.CompilerParams(
            collective_id=0, has_side_effects=True, vmem_limit_bytes=60 * 1024 * 1024
        ),
        name="detect",
    )(plan, template_ids.T, channel_mask, channel_mask.reshape(1, -1), records, bank)


def solution(mesh):
    placed = (
        P("groups", "tm"),
        P("tm", "groups", None),
        P("groups"),
        P("groups", None),
        P("groups"),
    )
    return jax.shard_map(
        shards, mesh=mesh, in_specs=placed, out_specs=P("groups", None, "tm"), check_vma=False
    )
```

```python
import functools

import jax
import jax.numpy as jnp
from jax import lax
from jax.experimental import pallas as pl
from jax.experimental.pallas import tpu as pltpu
from jax.sharding import PartitionSpec as P

MESH = pl.DeviceIdType.MESH
LANES = 128
DIRECT = 0


def up(value, unit):
    return -(-value // unit) * unit


def kernel(
    n, owners, steps, kk, taps,
    plan_in, ids_in, mask_in, row_in, rec_ref, bank_ref, out_ref,
    plan_ref, ids_ref, mask_s, mask_v, bank_v, tsend, tpart, tcomb, pair_in, pair_out, trecv, tpair, rrecv,
    xs, frames, inv, tmpl, wts, acc, osend, orecv,
    ready, few_sem, bank_sem, rs_sem, rr_sem, fs_sem, fr_sem, cs_sem, cr_sem, ps_sem, pr_sem, ts_sem, tr_sem,
    qs_sem, qr_sem, os_sem, or_sem,
):
    me = lax.axis_index("tm")
    chip, core = me // 2, me % 2
    chips = n // 2
    partner = me + 1 - 2 * core
    side = chip % 2
    twin = chip + 1 - 2 * side
    chans, block = rec_ref.shape
    own = chans // owners
    halves = block // LANES
    part = LANES // 2
    width = frames.shape[2] // LANES
    dims = (((1,), (1,)), ((), ()))
    direct = min(DIRECT, steps)
    paired = range(direct, steps)
    owner = chip < owners

    def tell(sem, to):
        pl.semaphore_signal(sem, inc=1, device_id={"tm": to}, device_id_type=MESH)

    def push(src, dst, send_sem, recv_sem, to):
        return pltpu.make_async_remote_copy(
            src_ref=src, dst_ref=dst, send_sem=send_sem, recv_sem=recv_sem,
            device_id={"tm": to}, device_id_type=MESH,
        )

    def sent(ref, sem):
        push(ref, ref, sem, sem, partner).wait_send()

    def landed(ref, sem):
        push(ref, ref, sem, sem, partner).wait_recv()

    fetch = pltpu.make_async_copy(bank_ref, bank_v, bank_sem)
    fetch.start()
    few = [
        pltpu.make_async_copy(src, dst, few_sem.at[i])
        for i, (src, dst) in enumerate([(plan_in, plan_ref), (ids_in, ids_ref), (mask_in, mask_s), (row_in, mask_v)])
    ]
    for copy in few:
        copy.start()
    barrier = pltpu.get_barrier_semaphore()
    tell(barrier, partner)

    @pl.loop(chip + 1, chips)
    def _(q):
        tell(barrier, 2 * q + core)

    pl.semaphore_wait(barrier, 1 + chip)
    lower = jnp.minimum(chip, owners)

    def rows_of(q):
        return rec_ref.at[pl.ds(pl.multiple_of(q * own, 8), own)]

    def send_records(q):
        return push(rows_of(q), rrecv.at[core, chip], rs_sem, rr_sem, 2 * q + core)

    def across(s):
        return push(tsend.at[s], tpart.at[s], cs_sem.at[s], cr_sem.at[s], partner)

    def spread(s, q):
        return push(tcomb.at[s, q % 2, q // 2], trecv[s].at[chip], ts_sem.at[s], tr_sem.at[s], 2 * q + core)

    def to_twin(s):
        at = s - direct
        return push(tcomb.at[s, 1 - side], pair_in.at[at], ps_sem.at[at], pr_sem.at[at], 2 * twin + core)

    def spread_pair(s, i):
        at = s - direct
        return push(
            pair_out.at[at, i], tpair[at].at[chip // 2], qs_sem.at[at], qr_sem.at[at], 2 * (2 * i + side) + core
        )

    for copy in few:
        copy.wait()
    fetch.wait()
    order = list(paired) + list(range(direct))
    for s in order:
        for j in range(kk):
            pick = bank_v[ids_ref[(1 - core) * kk + j, s]]
            for q in range(owners):
                tsend[s, q % 2, q // 2, j] = pick[q * own : (q + 1) * own]
        across(s).start()

    @pl.loop(0, chip)
    def _(q):
        tell(ready.at[chip], 2 * q + core)

    @pl.loop(0, lower)
    def _(q):
        send_records(q).start()

    for s in order:
        theirs = plan_ref[s] == partner
        across(s).wait_recv()
        for j in range(kk):
            pick = bank_v[ids_ref[core * kk + j, s]]
            for q in range(owners):
                at = (s, q % 2, q // 2, j)
                tcomb[at] = jnp.where(theirs, tpart[at], pick[q * own : (q + 1) * own])
        if s >= direct:
            if s == direct:

                @pl.when(twin > chip)
                def _():
                    pl.semaphore_wait(ready.at[twin], 1)

            to_twin(s).start()
        else:

            @pl.loop(0, lower)
            def _(q):
                spread(s, q).start()

    keep = pltpu.make_async_copy(rows_of(lax.rem(chip, owners)), rrecv.at[core, chip], bank_sem)
    keep.start()

    @pl.loop(chip + 1, owners)
    def _(q):
        @pl.when(q != twin)
        def _():
            pl.semaphore_wait(ready.at[q], 1)

        send_records(q).start()
        if direct:
            spread(0, q).start()

    for s in range(1, direct):

        @pl.loop(chip + 1, owners)
        def _(q):
            spread(s, q).start()

    for s in paired:
        at = s - direct
        landed(pair_in.at[at], pr_sem.at[at])
        theirs = lax.div(plan_ref[s], 2) == twin
        for i in range(owners // 2):
            pair_out[at, i] = jnp.where(theirs, pair_in[at, i], tcomb[s, side, i])

        @pl.loop(0, owners // 2)
        def _(i):
            @pl.when(i != chip // 2)
            def _():
                spread_pair(s, i).start()

    keep.wait()
    rows = steps * kk * halves
    others = pl.ds(0, chips - 1)

    @pl.when(owner)
    def _():
        for s in paired:
            tpair[s - direct][chip // 2] = pair_out[s - direct, lax.rem(chip // 2, owners // 2)]
        for s in range(direct):
            trecv[s][chip] = tcomb[s, side, lax.rem(chip // 2, owners // 2)]
        landed(rrecv.at[0, others], rr_sem)
        forward = push(rrecv.at[core], rrecv.at[core], fs_sem, fr_sem, partner)
        forward.start()
        forward.wait_recv()

        for v in range(halves):
            for a in range(n):
                xs[v, a * own : (a + 1) * own, :] = rrecv[a % 2, a // 2, :, v * LANES : (v + 1) * LANES].astype(
                    jnp.float32
                )
            xs[v, n * own :, :] = jnp.zeros((xs.shape[1] - n * own, LANES), jnp.float32)
        shift = lax.broadcasted_iota(jnp.int32, (part, width * LANES), 1) - lax.broadcasted_iota(
            jnp.int32, (part, width * LANES), 0
        )
        band = jnp.where((shift >= 0) & (shift < taps), 1.0, 0.0).astype(jnp.bfloat16)
        live = jnp.sum(mask_v[...].astype(jnp.float32), axis=1, keepdims=True)
        scale = jnp.sqrt(taps / (1.0 + live))
        left = lax.broadcasted_iota(jnp.int32, (n, LANES), 1) < part

        def frame(i, carry):
            tiles = [
                xs[q % halves, pl.ds(i + (q // halves) * own, n, stride=own), :] for q in range(halves + width)
            ]
            turned = [pltpu.roll(tile, part, 1) for tile in tiles]
            odd = [jnp.where(left, turned[q], turned[q + 1]) for q in range(halves + width - 1)]
            x = jnp.concatenate(
                [jnp.concatenate(some[h : h + width], axis=1) for some in (tiles, odd) for h in range(halves)], axis=0
            )
            frames[i] = x.astype(jnp.bfloat16)
            sq = x * x
            high = sq.astype(jnp.bfloat16)
            low = (sq - high.astype(jnp.float32)).astype(jnp.bfloat16)
            energy = lax.dot_general(
                jnp.concatenate([high, low], axis=0), band, dims, preferred_element_type=jnp.float32
            )
            energy = energy[: 2 * halves * n] + energy[2 * halves * n :]
            factor = scale * mask_s[chip * own + i].astype(jnp.float32)
            inv[i] = factor / jnp.sqrt(energy + 1e-06)
            return carry

        lax.fori_loop(0, own, frame, 0, unroll=own)

        for s in range(steps):
            if s >= direct:
                landed(tpair[s - direct].at[pl.ds(0, chips // 2 - 1)], qr_sem.at[s - direct])
            else:
                landed(trecv[s].at[others], tr_sem.at[s])
            for j in range(kk):
                if s >= direct:
                    got = tpair[s - direct][lax.div(plan_ref[s], 4), j]
                else:
                    got = trecv[s][lax.div(plan_ref[s], 2), j]
                got = got.astype(jnp.float32)
                tmpl[...] = jnp.concatenate([got, jnp.zeros((own, width * LANES - taps), jnp.float32)], axis=1)
                energy = jnp.sum(got * got, axis=1, keepdims=True)
                wts[...] = jnp.broadcast_to(1.0 / jnp.sqrt(energy + 1e-06), (own, part))

                def channel(i, total):
                    base = jnp.broadcast_to(tmpl[pl.ds(i, 1), :], (16, width * LANES)).astype(jnp.bfloat16)
                    base = jnp.concatenate([base] * (part // 16), axis=0)
                    taps_of = pltpu.roll(base, 0, 1, stride=1, stride_axis=0)
                    raw = lax.dot_general(frames[i], taps_of, dims, preferred_element_type=jnp.float32)
                    return total + raw * inv[i] * wts[pl.ds(i, 1), :]

                total = lax.fori_loop(0, own, channel, jnp.zeros((2 * halves * n, part), jnp.float32), unroll=own)
                total = jnp.concatenate([total[: halves * n], total[halves * n :]], axis=1)
                at = (s * kk + j) * halves * n
                acc[at : at + halves * n, :] = total

        for d in range(n):
            osend[d] = acc[pl.ds(d, rows, stride=n), :]
        orecv[me] = osend[me]

        @pl.loop(jnp.maximum(chip + 1, owners), chips)
        def _(q):
            @pl.when(q != twin)
            def _():
                pl.semaphore_wait(ready.at[q], 1)

        def give(d):
            return push(osend.at[d], orecv.at[me], os_sem, or_sem, d)

        @pl.loop(0, me)
        def _(d):
            give(d).start()

        @pl.loop(me + 1, n)
        def _(d):
            give(d).start()

        landed(orecv.at[pl.ds(0, 2 * owners - 1)], or_sem)

    @pl.when(jnp.logical_not(owner))
    def _():
        @pl.loop(chip + 1, chips)
        def _(q):
            @pl.when(q != twin)
            def _():
                pl.semaphore_wait(ready.at[q], 1)

        landed(orecv, or_sem)

    totals = jnp.sum(orecv[...].reshape(owners, 2, rows, LANES), axis=0)
    for c in range(2):
        for s in range(steps):
            for j in range(kk):
                for h in range(halves):
                    r = (s * kk + j) * halves + h
                    out_ref[s, c * kk + j, h * LANES : (h + 1) * LANES] = totals[c, r]

    for s in range(steps):
        across(s).wait_send()
    for s in paired:
        to_twin(s).wait_send()

    @pl.when(owner)
    def _():
        sent(rrecv.at[0, pl.ds(0, owners - 1)], rs_sem)
        push(rrecv.at[core], rrecv.at[core], fs_sem, fr_sem, partner).wait_send()
        sent(osend.at[pl.ds(0, n - 1)], os_sem)
        for s in paired:
            sent(pair_out.at[s - direct, pl.ds(0, owners // 2 - 1)], qs_sem.at[s - direct])
        for s in range(direct):
            sent(trecv[s].at[pl.ds(0, owners - 1)], ts_sem.at[s])

    @pl.when(jnp.logical_not(owner))
    def _():
        sent(rrecv.at[0, pl.ds(0, owners)], rs_sem)
        for s in paired:
            sent(pair_out.at[s - direct], qs_sem.at[s - direct])
        for s in range(direct):
            sent(trecv[s].at[pl.ds(0, owners)], ts_sem.at[s])


def shards(records, bank, plan, template_ids, channel_mask):
    n = lax.axis_size("tm")
    chips = n // 2
    owners = chips
    steps, kcount = template_ids.shape
    chans, block = records.shape
    slots, _, taps = bank.shape
    kk = kcount // 2
    own = up(-(-chans // owners), 8)
    if own * owners != chans:
        more = own * owners - chans
        records = jnp.pad(records, ((0, more), (0, 0)))
        bank = jnp.pad(bank, ((0, 0), (0, more), (0, 0)))
        channel_mask = jnp.pad(channel_mask, (0, more))
    halves = block // LANES
    part = LANES // 2
    width = up(part + taps - 1, LANES) // LANES
    vmem = pl.BlockSpec(memory_space=pltpu.VMEM)
    hbm = pl.BlockSpec(memory_space=pl.ANY)
    f32, bf16 = jnp.float32, jnp.bfloat16
    dma = pltpu.SemaphoreType.DMA
    extra = -(-(halves + width - 1) // halves)
    rows = steps * kk * halves
    piece = (kk, own, taps)
    direct = min(DIRECT, steps)
    return pl.pallas_call(
        functools.partial(kernel, n, owners, steps, kk, taps),
        out_shape=jax.ShapeDtypeStruct((steps, kcount, block), f32),
        in_specs=[hbm] * 6,
        out_specs=vmem,
        scratch_shapes=[
            pltpu.SMEM((steps,), jnp.int32),
            pltpu.SMEM((kcount, steps), jnp.int32),
            pltpu.SMEM(channel_mask.shape, jnp.int32),
            pltpu.VMEM((1, channel_mask.shape[0]), jnp.int32),
            pltpu.VMEM(bank.shape, bf16),
            pltpu.VMEM((steps, 2, owners // 2, *piece), bf16),
            pltpu.VMEM((steps, 2, owners // 2, *piece), bf16),
            pltpu.VMEM((steps, 2, owners // 2, *piece), bf16),
            pltpu.VMEM((max(steps - direct, 1), owners // 2, *piece), bf16),
            pltpu.VMEM((max(steps - direct, 1), owners // 2, *piece), bf16),
            [pltpu.VMEM((chips, *piece), bf16)] * direct,
            [pltpu.VMEM((chips // 2, *piece), bf16)] * (steps - direct),
            pltpu.VMEM((2, chips, own, block), bf16),
            pltpu.VMEM((halves, (n + extra) * own, LANES), f32),
            pltpu.VMEM((own, 2 * halves * n, width * LANES), bf16),
            pltpu.VMEM((own, 2 * halves * n, part), f32),
            pltpu.VMEM((own, width * LANES), f32),
            pltpu.VMEM((own, part), f32),
            pltpu.VMEM((rows * n, LANES), f32),
            pltpu.VMEM((n, rows, LANES), f32),
            pltpu.VMEM((2 * owners, rows, LANES), f32),
            pltpu.SemaphoreType.REGULAR((chips,)),
            dma((4,)), dma(()), dma(()), dma(()), dma(()), dma(()), dma((steps,)), dma((steps,)), dma((max(steps - direct, 1),)), dma((max(steps - direct, 1),)),
            dma((max(direct, 1),)), dma((max(direct, 1),)), dma((max(steps - direct, 1),)), dma((max(steps - direct, 1),)), dma(()), dma(()),
        ],
        compiler_params=pltpu.CompilerParams(
            collective_id=0, has_side_effects=True, vmem_limit_bytes=60 * 1024 * 1024
        ),
        name="detect",
    )(plan, template_ids.T, channel_mask, channel_mask.reshape(1, -1), records, bank)


def solution(mesh):
    placed = (
        P("groups", "tm"),
        P("tm", "groups", None),
        P("groups"),
        P("groups", None),
        P("groups"),
    )
    return jax.shard_map(
        shards, mesh=mesh, in_specs=placed, out_specs=P("groups", None, "tm"), check_vma=False
    )
```

```python
import functools

import jax
import jax.numpy as jnp
from jax import lax
from jax.experimental import pallas as pl
from jax.experimental.pallas import tpu as pltpu
from jax.sharding import PartitionSpec as P

MESH = pl.DeviceIdType.MESH
LANES = 128
ALONG = (1, 0, 0)
ORDER = (0, 1, 2)


def up(value, unit):
    return -(-value // unit) * unit


def kernel(
    n, steps, kk, taps,
    plan_in, ids_in, mask_in, row_in, rec_ref, bank_ref, out_ref,
    plan_ref, ids_ref, mask_s, mask_v, bank_v, tsend, tpart, tcomb, pair_in, pair_out, tpair, rrecv,
    xs, frames, inv, tmpl, wts, acc, osend, orecv,
    ready, few_sem, bank_sem, rs_sem, rr_sem, fs_sem, fr_sem, cs_sem, cr_sem, ps_sem, pr_sem,
    qs_sem, qr_sem, os_sem, or_sem,
):
    me = lax.axis_index("tm")
    chip, core = me // 2, me % 2
    chips = n // 2
    partner = me + 1 - 2 * core
    chans, block = rec_ref.shape
    own = chans // chips
    halves = block // LANES
    part = LANES // 2
    width = frames.shape[2] // LANES
    dims = (((1,), (1,)), ((), ()))
    along = [ALONG[s % len(ALONG)] for s in range(steps)]
    order = sorted(range(steps), key=lambda s: ORDER[s % len(ORDER)])

    def side(s, q):
        return q // (1 + along[s]) % 2

    def place(s, q):
        return q // 4 * 2 + q % 2 if along[s] else q // 2

    def chip_at(s, i):
        return i // 2 * 4 + side(s, chip) * 2 + i % 2 if along[s] else i * 2 + side(s, chip)

    def twin(s):
        return chip + (1 - 2 * side(s, chip)) * (1 + along[s])


    def tell(sem, to):
        pl.semaphore_signal(sem, inc=1, device_id={"tm": to}, device_id_type=MESH)

    def push(src, dst, send_sem, recv_sem, to):
        return pltpu.make_async_remote_copy(
            src_ref=src, dst_ref=dst, send_sem=send_sem, recv_sem=recv_sem,
            device_id={"tm": to}, device_id_type=MESH,
        )

    def sent(ref, sem):
        push(ref, ref, sem, sem, partner).wait_send()

    def landed(ref, sem):
        push(ref, ref, sem, sem, partner).wait_recv()

    fetch = pltpu.make_async_copy(bank_ref, bank_v, bank_sem)
    fetch.start()
    few = [
        pltpu.make_async_copy(src, dst, few_sem.at[i])
        for i, (src, dst) in enumerate([(plan_in, plan_ref), (ids_in, ids_ref), (mask_in, mask_s), (row_in, mask_v)])
    ]
    for copy in few:
        copy.start()
    barrier = pltpu.get_barrier_semaphore()
    tell(barrier, partner)

    @pl.loop(chip + 1, chips)
    def _(q):
        tell(barrier, 2 * q + core)

    pl.semaphore_wait(barrier, 1 + chip)
    def rows_of(q):
        return rec_ref.at[pl.ds(pl.multiple_of(q * own, 8), own)]

    def send_records(q):
        return push(rows_of(q), rrecv.at[core, chip], rs_sem, rr_sem, 2 * q + core)

    def across(s):
        return push(tsend.at[s], tpart.at[s], cs_sem.at[s], cr_sem.at[s], partner)

    def to_twin(s):
        return push(tcomb.at[s, 1 - side(s, chip)], pair_in.at[s], ps_sem.at[s], pr_sem.at[s], 2 * twin(s) + core)

    def spread(s, i):
        return push(
            pair_out.at[s, i], tpair[s].at[place(s, chip)], qs_sem.at[s], qr_sem.at[s], 2 * chip_at(s, i) + core
        )

    for copy in few:
        copy.wait()
    fetch.wait()
    for s in order:
        for j in range(kk):
            pick = bank_v[ids_ref[(1 - core) * kk + j, s]]
            for q in range(chips):
                tsend[s, side(s, q), place(s, q), j] = pick[q * own : (q + 1) * own]
        across(s).start()

    @pl.loop(0, chip)
    def _(q):
        tell(ready.at[chip], 2 * q + core)

    @pl.loop(0, chip)
    def _(q):
        send_records(q).start()

    for s in order:
        theirs = plan_ref[s] == partner
        across(s).wait_recv()
        for j in range(kk):
            pick = bank_v[ids_ref[core * kk + j, s]]
            for q in range(chips):
                at = (s, side(s, q), place(s, q), j)
                tcomb[at] = jnp.where(theirs, tpart[at], pick[q * own : (q + 1) * own])
        if s == min(order, key=lambda t: (along[t] != along[s], order.index(t))):

            @pl.when(twin(s) > chip)
            def _():
                pl.semaphore_wait(ready.at[twin(s)], 1)

        to_twin(s).start()

    keep = pltpu.make_async_copy(rows_of(chip), rrecv.at[core, chip], bank_sem)
    keep.start()

    met = [order[0]] + [s for s in order if along[s] != along[order[0]]][:1]

    @pl.loop(chip + 1, chips)
    def _(q):
        fresh = functools.reduce(jnp.logical_and, [q != twin(s) for s in met])

        @pl.when(fresh)
        def _():
            pl.semaphore_wait(ready.at[q], 1)

        send_records(q).start()

    for s in order:
        landed(pair_in.at[s], pr_sem.at[s])
        theirs = lax.div(plan_ref[s], 2) == twin(s)
        for i in range(chips // 2):
            pair_out[s, i] = jnp.where(theirs, pair_in[s, i], tcomb[s, side(s, chip), i])

        @pl.loop(0, chips // 2)
        def _(i):
            @pl.when(i != place(s, chip))
            def _():
                spread(s, i).start()

    keep.wait()
    rows = steps * kk * halves
    others = pl.ds(0, chips - 1)

    for s in range(steps):
        tpair[s][place(s, chip)] = pair_out[s, place(s, chip)]
    landed(rrecv.at[0, others], rr_sem)
    forward = push(rrecv.at[core], rrecv.at[core], fs_sem, fr_sem, partner)
    forward.start()
    forward.wait_recv()

    for v in range(halves):
        for a in range(n):
            xs[v, a * own : (a + 1) * own, :] = rrecv[a % 2, a // 2, :, v * LANES : (v + 1) * LANES].astype(
                jnp.float32
            )
        xs[v, n * own :, :] = jnp.zeros((xs.shape[1] - n * own, LANES), jnp.float32)
    shift = lax.broadcasted_iota(jnp.int32, (part, width * LANES), 1) - lax.broadcasted_iota(
        jnp.int32, (part, width * LANES), 0
    )
    band = jnp.where((shift >= 0) & (shift < taps), 1.0, 0.0).astype(jnp.bfloat16)
    live = jnp.sum(mask_v[...].astype(jnp.float32), axis=1, keepdims=True)
    scale = jnp.sqrt(taps / (1.0 + live))
    left = lax.broadcasted_iota(jnp.int32, (n, LANES), 1) < part

    def frame(i, carry):
        tiles = [
            xs[q % halves, pl.ds(i + (q // halves) * own, n, stride=own), :] for q in range(halves + width)
        ]
        turned = [pltpu.roll(tile, part, 1) for tile in tiles]
        odd = [jnp.where(left, turned[q], turned[q + 1]) for q in range(halves + width - 1)]
        x = jnp.concatenate(
            [jnp.concatenate(some[h : h + width], axis=1) for some in (tiles, odd) for h in range(halves)], axis=0
        )
        frames[i] = x.astype(jnp.bfloat16)
        sq = x * x
        high = sq.astype(jnp.bfloat16)
        low = (sq - high.astype(jnp.float32)).astype(jnp.bfloat16)
        energy = lax.dot_general(
            jnp.concatenate([high, low], axis=0), band, dims, preferred_element_type=jnp.float32
        )
        energy = energy[: 2 * halves * n] + energy[2 * halves * n :]
        factor = scale * mask_s[chip * own + i].astype(jnp.float32)
        inv[i] = factor / jnp.sqrt(energy + 1e-06)
        return carry

    lax.fori_loop(0, own, frame, 0, unroll=own)

    for s in order:
        landed(tpair[s].at[pl.ds(0, chips // 2 - 1)], qr_sem.at[s])
        for j in range(kk):
            got = tpair[s][place(s, lax.div(plan_ref[s], 2)), j]
            got = got.astype(jnp.float32)
            tmpl[...] = jnp.concatenate([got, jnp.zeros((own, width * LANES - taps), jnp.float32)], axis=1)
            energy = jnp.sum(got * got, axis=1, keepdims=True)
            wts[...] = jnp.broadcast_to(1.0 / jnp.sqrt(energy + 1e-06), (own, part))

            def channel(i, total):
                base = jnp.broadcast_to(tmpl[pl.ds(i, 1), :], (16, width * LANES)).astype(jnp.bfloat16)
                base = jnp.concatenate([base] * (part // 16), axis=0)
                taps_of = pltpu.roll(base, 0, 1, stride=1, stride_axis=0)
                raw = lax.dot_general(frames[i], taps_of, dims, preferred_element_type=jnp.float32)
                return total + raw * inv[i] * wts[pl.ds(i, 1), :]

            total = lax.fori_loop(0, own, channel, jnp.zeros((2 * halves * n, part), jnp.float32), unroll=own)
            total = jnp.concatenate([total[: halves * n], total[halves * n :]], axis=1)
            at = (s * kk + j) * halves * n
            acc[at : at + halves * n, :] = total

    for d in range(n):
        osend[d] = acc[pl.ds(d, rows, stride=n), :]
    orecv[me] = osend[me]

    def give(d):
        return push(osend.at[d], orecv.at[me], os_sem, or_sem, d)

    @pl.loop(0, me)
    def _(d):
        give(d).start()

    @pl.loop(me + 1, n)
    def _(d):
        give(d).start()

    landed(orecv.at[pl.ds(0, n - 1)], or_sem)

    totals = jnp.sum(orecv[...].reshape(chips, 2, rows, LANES), axis=0)
    for c in range(2):
        for s in range(steps):
            for j in range(kk):
                for h in range(halves):
                    r = (s * kk + j) * halves + h
                    out_ref[s, c * kk + j, h * LANES : (h + 1) * LANES] = totals[c, r]

    for s in range(steps):
        across(s).wait_send()
        to_twin(s).wait_send()
        sent(pair_out.at[s, pl.ds(0, chips // 2 - 1)], qs_sem.at[s])
    sent(rrecv.at[0, others], rs_sem)
    forward.wait_send()
    sent(osend.at[pl.ds(0, n - 1)], os_sem)


def shards(records, bank, plan, template_ids, channel_mask):
    n = lax.axis_size("tm")
    chips = n // 2
    steps, kcount = template_ids.shape
    chans, block = records.shape
    slots, _, taps = bank.shape
    kk = kcount // 2
    own = up(-(-chans // chips), 8)
    if own * chips != chans:
        more = own * chips - chans
        records = jnp.pad(records, ((0, more), (0, 0)))
        bank = jnp.pad(bank, ((0, 0), (0, more), (0, 0)))
        channel_mask = jnp.pad(channel_mask, (0, more))
    halves = block // LANES
    part = LANES // 2
    width = up(part + taps - 1, LANES) // LANES
    vmem = pl.BlockSpec(memory_space=pltpu.VMEM)
    hbm = pl.BlockSpec(memory_space=pl.ANY)
    f32, bf16 = jnp.float32, jnp.bfloat16
    dma = pltpu.SemaphoreType.DMA
    extra = -(-(halves + width - 1) // halves)
    rows = steps * kk * halves
    piece = (kk, own, taps)
    return pl.pallas_call(
        functools.partial(kernel, n, steps, kk, taps),
        out_shape=jax.ShapeDtypeStruct((steps, kcount, block), f32),
        in_specs=[hbm] * 6,
        out_specs=vmem,
        scratch_shapes=[
            pltpu.SMEM((steps,), jnp.int32),
            pltpu.SMEM((kcount, steps), jnp.int32),
            pltpu.SMEM(channel_mask.shape, jnp.int32),
            pltpu.VMEM((1, channel_mask.shape[0]), jnp.int32),
            pltpu.VMEM(bank.shape, bf16),
            pltpu.VMEM((steps, 2, chips // 2, *piece), bf16),
            pltpu.VMEM((steps, 2, chips // 2, *piece), bf16),
            pltpu.VMEM((steps, 2, chips // 2, *piece), bf16),
            pltpu.VMEM((steps, chips // 2, *piece), bf16),
            pltpu.VMEM((steps, chips // 2, *piece), bf16),
            [pltpu.VMEM((chips // 2, *piece), bf16)] * steps,
            pltpu.VMEM((2, chips, own, block), bf16),
            pltpu.VMEM((halves, (n + extra) * own, LANES), f32),
            pltpu.VMEM((own, 2 * halves * n, width * LANES), bf16),
            pltpu.VMEM((own, 2 * halves * n, part), f32),
            pltpu.VMEM((own, width * LANES), f32),
            pltpu.VMEM((own, part), f32),
            pltpu.VMEM((rows * n, LANES), f32),
            pltpu.VMEM((n, rows, LANES), f32),
            pltpu.VMEM((2 * chips, rows, LANES), f32),
            pltpu.SemaphoreType.REGULAR((chips,)),
            dma((4,)), dma(()), dma(()), dma(()), dma(()), dma(()), dma((steps,)), dma((steps,)), dma((steps,)),
            dma((steps,)), dma((steps,)), dma((steps,)), dma(()), dma(()),
        ],
        compiler_params=pltpu.CompilerParams(
            collective_id=0, has_side_effects=True, vmem_limit_bytes=60 * 1024 * 1024
        ),
        name="detect",
    )(plan, template_ids.T, channel_mask, channel_mask.reshape(1, -1), records, bank)


def solution(mesh):
    placed = (
        P("groups", "tm"),
        P("tm", "groups", None),
        P("groups"),
        P("groups", None),
        P("groups"),
    )
    return jax.shard_map(
        shards, mesh=mesh, in_specs=placed, out_specs=P("groups", None, "tm"), check_vma=False
    )
```

```python
import functools

import jax
import jax.numpy as jnp
from jax import lax
from jax.experimental import pallas as pl
from jax.experimental.pallas import tpu as pltpu
from jax.sharding import PartitionSpec as P

MESH = pl.DeviceIdType.MESH
LANES = 128
ALONG = (1, 0, 0)
ORDER = (0, 1, 2)


def up(value, unit):
    return -(-value // unit) * unit


def kernel(
    n, steps, kk, taps,
    plan_in, ids_in, mask_in, row_in, rec_ref, bank_ref, out_ref,
    plan_ref, ids_ref, mask_s, mask_v, bank_v, tsend, tpart, tcomb, pair_in, pair_out, tpair, rrecv,
    xs, frames, inv, tmpl, wts, acc, osend,
    ready, few_sem, bank_sem, rs_sem, rr_sem, fs_sem, fr_sem, cs_sem, cr_sem, ps_sem, pr_sem,
    qs_sem, qr_sem, os_sem, or_sem,
):
    me = lax.axis_index("tm")
    chip, core = me // 2, me % 2
    chips = n // 2
    partner = me + 1 - 2 * core
    chans, block = rec_ref.shape
    own = chans // chips
    halves = block // LANES
    part = LANES // 2
    width = frames.shape[2] // LANES
    dims = (((1,), (1,)), ((), ()))
    along = [ALONG[s % len(ALONG)] for s in range(steps)]
    order = sorted(range(steps), key=lambda s: ORDER[s % len(ORDER)])

    def side(s, q):
        return q // (1 + along[s]) % 2

    def place(s, q):
        return q // 4 * 2 + q % 2 if along[s] else q // 2

    def chip_at(s, i):
        return i // 2 * 4 + side(s, chip) * 2 + i % 2 if along[s] else i * 2 + side(s, chip)

    def twin(s):
        return chip + (1 - 2 * side(s, chip)) * (1 + along[s])


    def tell(sem, to):
        pl.semaphore_signal(sem, inc=1, device_id={"tm": to}, device_id_type=MESH)

    def push(src, dst, send_sem, recv_sem, to):
        return pltpu.make_async_remote_copy(
            src_ref=src, dst_ref=dst, send_sem=send_sem, recv_sem=recv_sem,
            device_id={"tm": to}, device_id_type=MESH,
        )

    def sent(ref, sem):
        push(ref, ref, sem, sem, partner).wait_send()

    def landed(ref, sem):
        push(ref, ref, sem, sem, partner).wait_recv()

    fetch = pltpu.make_async_copy(bank_ref, bank_v, bank_sem)
    fetch.start()
    few = [
        pltpu.make_async_copy(src, dst, few_sem.at[i])
        for i, (src, dst) in enumerate([(plan_in, plan_ref), (ids_in, ids_ref), (mask_in, mask_s), (row_in, mask_v)])
    ]
    for copy in few:
        copy.start()
    barrier = pltpu.get_barrier_semaphore()
    tell(barrier, partner)

    @pl.loop(chip + 1, chips)
    def _(q):
        tell(barrier, 2 * q + core)

    pl.semaphore_wait(barrier, 1 + chip)
    def rows_of(q):
        return rec_ref.at[pl.ds(pl.multiple_of(q * own, 8), own)]

    def send_records(q):
        return push(rows_of(q), rrecv.at[core, chip], rs_sem, rr_sem, 2 * q + core)

    def across(s):
        return push(tsend.at[s], tpart.at[s], cs_sem.at[s], cr_sem.at[s], partner)

    def to_twin(s):
        return push(tcomb.at[s, 1 - side(s, chip)], pair_in.at[s], ps_sem.at[s], pr_sem.at[s], 2 * twin(s) + core)

    def spread(s, i):
        return push(
            pair_out.at[s, i], tpair[s].at[place(s, chip)], qs_sem.at[s], qr_sem.at[s], 2 * chip_at(s, i) + core
        )

    for copy in few:
        copy.wait()
    fetch.wait()
    for s in order:
        for j in range(kk):
            pick = bank_v[ids_ref[(1 - core) * kk + j, s]]
            for q in range(chips):
                tsend[s, side(s, q), place(s, q), j] = pick[q * own : (q + 1) * own]
        across(s).start()

    @pl.loop(0, chip)
    def _(q):
        tell(ready.at[chip], 2 * q + core)

    @pl.loop(0, chip)
    def _(q):
        send_records(q).start()

    for s in order:
        theirs = plan_ref[s] == partner
        across(s).wait_recv()
        for j in range(kk):
            pick = bank_v[ids_ref[core * kk + j, s]]
            for q in range(chips):
                at = (s, side(s, q), place(s, q), j)
                tcomb[at] = jnp.where(theirs, tpart[at], pick[q * own : (q + 1) * own])
        if s == min(order, key=lambda t: (along[t] != along[s], order.index(t))):

            @pl.when(twin(s) > chip)
            def _():
                pl.semaphore_wait(ready.at[twin(s)], 1)

        to_twin(s).start()

    keep = pltpu.make_async_copy(rows_of(chip), rrecv.at[core, chip], bank_sem)
    keep.start()

    met = [order[0]] + [s for s in order if along[s] != along[order[0]]][:1]

    @pl.loop(chip + 1, chips)
    def _(q):
        fresh = functools.reduce(jnp.logical_and, [q != twin(s) for s in met])

        @pl.when(fresh)
        def _():
            pl.semaphore_wait(ready.at[q], 1)

        send_records(q).start()

    for s in order:
        landed(pair_in.at[s], pr_sem.at[s])
        theirs = lax.div(plan_ref[s], 2) == twin(s)
        for i in range(chips // 2):
            pair_out[s, i] = jnp.where(theirs, pair_in[s, i], tcomb[s, side(s, chip), i])

        @pl.loop(0, chips // 2)
        def _(i):
            @pl.when(i != place(s, chip))
            def _():
                spread(s, i).start()

    keep.wait()
    rows = steps * kk
    others = pl.ds(0, chips - 1)

    for s in range(steps):
        tpair[s][place(s, chip)] = pair_out[s, place(s, chip)]
    landed(rrecv.at[0, others], rr_sem)
    forward = push(rrecv.at[core], rrecv.at[core], fs_sem, fr_sem, partner)
    forward.start()
    forward.wait_recv()

    for v in range(halves):
        for a in range(n):
            xs[v, a * own : (a + 1) * own, :] = rrecv[a % 2, a // 2, :, v * LANES : (v + 1) * LANES].astype(
                jnp.float32
            )
        xs[v, n * own :, :] = jnp.zeros((xs.shape[1] - n * own, LANES), jnp.float32)
    shift = lax.broadcasted_iota(jnp.int32, (part, width * LANES), 1) - lax.broadcasted_iota(
        jnp.int32, (part, width * LANES), 0
    )
    band = jnp.where((shift >= 0) & (shift < taps), 1.0, 0.0).astype(jnp.bfloat16)
    live = jnp.sum(mask_v[...].astype(jnp.float32), axis=1, keepdims=True)
    scale = jnp.sqrt(taps / (1.0 + live))
    left = lax.broadcasted_iota(jnp.int32, (n, LANES), 1) < part

    def frame(i, carry):
        tiles = [
            xs[q % halves, pl.ds(i + (q // halves) * own, n, stride=own), :] for q in range(halves + width)
        ]
        turned = [pltpu.roll(tile, part, 1) for tile in tiles]
        odd = [jnp.where(left, turned[q], turned[q + 1]) for q in range(halves + width - 1)]
        x = jnp.concatenate(
            [jnp.concatenate(some[h : h + width], axis=1) for some in (tiles, odd) for h in range(halves)], axis=0
        )
        frames[i] = x.astype(jnp.bfloat16)
        sq = x * x
        high = sq.astype(jnp.bfloat16)
        low = (sq - high.astype(jnp.float32)).astype(jnp.bfloat16)
        energy = lax.dot_general(
            jnp.concatenate([high, low], axis=0), band, dims, preferred_element_type=jnp.float32
        )
        energy = energy[: 2 * halves * n] + energy[2 * halves * n :]
        factor = scale * mask_s[chip * own + i].astype(jnp.float32)
        inv[i] = factor / jnp.sqrt(energy + 1e-06)
        return carry

    lax.fori_loop(0, own, frame, 0, unroll=own)

    for s in order:
        landed(tpair[s].at[pl.ds(0, chips // 2 - 1)], qr_sem.at[s])
        for j in range(kk):
            got = tpair[s][place(s, lax.div(plan_ref[s], 2)), j]
            got = got.astype(jnp.float32)
            tmpl[...] = jnp.concatenate([got, jnp.zeros((own, width * LANES - taps), jnp.float32)], axis=1)
            energy = jnp.sum(got * got, axis=1, keepdims=True)
            wts[...] = jnp.broadcast_to(1.0 / jnp.sqrt(energy + 1e-06), (own, part))

            def channel(i, total):
                base = jnp.broadcast_to(tmpl[pl.ds(i, 1), :], (16, width * LANES)).astype(jnp.bfloat16)
                base = jnp.concatenate([base] * (part // 16), axis=0)
                taps_of = pltpu.roll(base, 0, 1, stride=1, stride_axis=0)
                raw = lax.dot_general(frames[i], taps_of, dims, preferred_element_type=jnp.float32)
                return total + raw * inv[i] * wts[pl.ds(i, 1), :]

            total = lax.fori_loop(0, own, channel, jnp.zeros((2 * halves * n, part), jnp.float32), unroll=own)
            total = jnp.concatenate([total[: halves * n], total[halves * n :]], axis=1)
            at = (s * kk + j) * halves * n
            acc[at : at + halves * n, :] = total

    for d in range(n):
        for h in range(halves):
            osend[d, :, h * LANES : (h + 1) * LANES] = acc[pl.ds(h * n + d, rows, stride=halves * n), :]

    def give(d):
        return push(osend.at[d], out_ref.at[core * chips + chip], os_sem, or_sem, d)

    @pl.loop(0, me)
    def _(d):
        give(d).start()

    @pl.loop(me + 1, n)
    def _(d):
        give(d).start()

    mine = pltpu.make_async_copy(osend.at[me], out_ref.at[core * chips + chip], bank_sem)
    mine.start()
    for s in range(steps):
        across(s).wait_send()
        to_twin(s).wait_send()
        sent(pair_out.at[s, pl.ds(0, chips // 2 - 1)], qs_sem.at[s])
    sent(rrecv.at[0, others], rs_sem)
    forward.wait_send()
    sent(osend.at[pl.ds(0, n - 1)], os_sem)
    mine.wait()
    landed(out_ref.at[pl.ds(0, n - 1)], or_sem)


def shards(records, bank, plan, template_ids, channel_mask):
    n = lax.axis_size("tm")
    chips = n // 2
    steps, kcount = template_ids.shape
    chans, block = records.shape
    slots, _, taps = bank.shape
    kk = kcount // 2
    own = up(-(-chans // chips), 8)
    if own * chips != chans:
        more = own * chips - chans
        records = jnp.pad(records, ((0, more), (0, 0)))
        bank = jnp.pad(bank, ((0, 0), (0, more), (0, 0)))
        channel_mask = jnp.pad(channel_mask, (0, more))
    halves = block // LANES
    part = LANES // 2
    width = up(part + taps - 1, LANES) // LANES
    hbm = pl.BlockSpec(memory_space=pl.ANY)
    f32, bf16 = jnp.float32, jnp.bfloat16
    dma = pltpu.SemaphoreType.DMA
    extra = -(-(halves + width - 1) // halves)
    rows = steps * kk
    piece = (kk, own, taps)
    parts = pl.pallas_call(
        functools.partial(kernel, n, steps, kk, taps),
        out_shape=jax.ShapeDtypeStruct((n, rows, block), f32),
        in_specs=[hbm] * 6,
        out_specs=hbm,
        scratch_shapes=[
            pltpu.SMEM((steps,), jnp.int32),
            pltpu.SMEM((kcount, steps), jnp.int32),
            pltpu.SMEM(channel_mask.shape, jnp.int32),
            pltpu.VMEM((1, channel_mask.shape[0]), jnp.int32),
            pltpu.VMEM(bank.shape, bf16),
            pltpu.VMEM((steps, 2, chips // 2, *piece), bf16),
            pltpu.VMEM((steps, 2, chips // 2, *piece), bf16),
            pltpu.VMEM((steps, 2, chips // 2, *piece), bf16),
            pltpu.VMEM((steps, chips // 2, *piece), bf16),
            pltpu.VMEM((steps, chips // 2, *piece), bf16),
            [pltpu.VMEM((chips // 2, *piece), bf16)] * steps,
            pltpu.VMEM((2, chips, own, block), bf16),
            pltpu.VMEM((halves, (n + extra) * own, LANES), f32),
            pltpu.VMEM((own, 2 * halves * n, width * LANES), bf16),
            pltpu.VMEM((own, 2 * halves * n, part), f32),
            pltpu.VMEM((own, width * LANES), f32),
            pltpu.VMEM((own, part), f32),
            pltpu.VMEM((rows * halves * n, LANES), f32),
            pltpu.VMEM((n, rows, block), f32),
            pltpu.SemaphoreType.REGULAR((chips,)),
            dma((4,)), dma(()), dma(()), dma(()), dma(()), dma(()), dma((steps,)), dma((steps,)), dma((steps,)),
            dma((steps,)), dma((steps,)), dma((steps,)), dma(()), dma(()),
        ],
        compiler_params=pltpu.CompilerParams(
            collective_id=0, has_side_effects=True, vmem_limit_bytes=60 * 1024 * 1024
        ),
        name="detect",
    )(plan, template_ids.T, channel_mask, channel_mask.reshape(1, -1), records, bank)
    sums = jnp.sum(parts.reshape(2, chips, steps, kk, block), axis=1)
    return jnp.swapaxes(sums, 0, 1).reshape(steps, kcount, block)


def solution(mesh):
    placed = (
        P("groups", "tm"),
        P("tm", "groups", None),
        P("groups"),
        P("groups", None),
        P("groups"),
    )
    return jax.shard_map(
        shards, mesh=mesh, in_specs=placed, out_specs=P("groups", None, "tm"), check_vma=False
    )
```

```python
import functools

import jax
import jax.numpy as jnp
from jax import lax
from jax.experimental import pallas as pl
from jax.experimental.pallas import tpu as pltpu
from jax.sharding import PartitionSpec as P

MESH = pl.DeviceIdType.MESH
LANES = 128
ALONG = (1, 0, 0)
ORDER = (0, 1, 2)


def up(value, unit):
    return -(-value // unit) * unit


def kernel(
    n, steps, kk, taps,
    plan_in, ids_in, mask_in, row_in, rec_ref, bank_ref, out_ref,
    plan_ref, ids_ref, mask_s, mask_v, bank_v, tsend, tpart, tcomb, pair_in, pair_out, tpair, rrecv,
    xs, frames, inv, tmpl, wts, acc, osend,
    ready, few_sem, bank_sem, rs_sem, rr_sem, fs_sem, fr_sem, cs_sem, cr_sem, ps_sem, pr_sem,
    qs_sem, qr_sem, os_sem, or_sem,
):
    me = lax.axis_index("tm")
    chip, core = me // 2, me % 2
    chips = n // 2
    partner = me + 1 - 2 * core
    chans, block = rec_ref.shape
    own = chans // chips
    halves = block // LANES
    part = LANES // 2
    width = frames.shape[2] // LANES
    dims = (((1,), (1,)), ((), ()))
    along = [ALONG[s % len(ALONG)] for s in range(steps)]
    order = sorted(range(steps), key=lambda s: ORDER[s % len(ORDER)])

    def side(s, q):
        return q // (1 + along[s]) % 2

    def place(s, q):
        return q // 4 * 2 + q % 2 if along[s] else q // 2

    def chip_at(s, i):
        return i // 2 * 4 + side(s, chip) * 2 + i % 2 if along[s] else i * 2 + side(s, chip)

    def twin(s):
        return chip + (1 - 2 * side(s, chip)) * (1 + along[s])


    def tell(sem, to):
        pl.semaphore_signal(sem, inc=1, device_id={"tm": to}, device_id_type=MESH)

    def push(src, dst, send_sem, recv_sem, to):
        return pltpu.make_async_remote_copy(
            src_ref=src, dst_ref=dst, send_sem=send_sem, recv_sem=recv_sem,
            device_id={"tm": to}, device_id_type=MESH,
        )

    def sent(ref, sem):
        push(ref, ref, sem, sem, partner).wait_send()

    def landed(ref, sem):
        push(ref, ref, sem, sem, partner).wait_recv()

    fetch = pltpu.make_async_copy(bank_ref, bank_v, bank_sem)
    fetch.start()
    few = [
        pltpu.make_async_copy(src, dst, few_sem.at[i])
        for i, (src, dst) in enumerate([(plan_in, plan_ref), (ids_in, ids_ref), (mask_in, mask_s), (row_in, mask_v)])
    ]
    for copy in few:
        copy.start()
    barrier = pltpu.get_barrier_semaphore()
    tell(barrier, partner)

    @pl.loop(chip + 1, chips)
    def _(q):
        tell(barrier, 2 * q + core)

    pl.semaphore_wait(barrier, 1 + chip)
    def rows_of(q):
        return rec_ref.at[pl.ds(pl.multiple_of(q * own, 8), own)]

    def send_records(q):
        return push(rows_of(q), rrecv.at[core, chip], rs_sem, rr_sem, 2 * q + core)

    def across(s):
        return push(tsend.at[s], tpart.at[s], cs_sem, cr_sem.at[s], partner)

    def to_twin(s):
        return push(tcomb.at[s, 1 - side(s, chip)], pair_in.at[s], ps_sem, pr_sem.at[s], 2 * twin(s) + core)

    def spread(s, i):
        return push(
            pair_out.at[s, i], tpair[s].at[place(s, chip)], qs_sem, qr_sem.at[s], 2 * chip_at(s, i) + core
        )

    @pl.loop(0, chip)
    def _(q):
        tell(ready.at[chip], 2 * q + core)

    for copy in few:
        copy.wait()
    fetch.wait()
    for s in order:
        for j in range(kk):
            pick = bank_v[ids_ref[(1 - core) * kk + j, s]]
            for q in range(chips):
                tsend[s, side(s, q), place(s, q), j] = pick[q * own : (q + 1) * own]
        across(s).start()

    @pl.loop(0, chip)
    def _(q):
        send_records(q).start()

    for s in order:
        theirs = plan_ref[s] == partner
        across(s).wait_recv()
        for j in range(kk):
            pick = bank_v[ids_ref[core * kk + j, s]]
            for q in range(chips):
                at = (s, side(s, q), place(s, q), j)
                tcomb[at] = jnp.where(theirs, tpart[at], pick[q * own : (q + 1) * own])
        if s == min(order, key=lambda t: (along[t] != along[s], order.index(t))):

            @pl.when(twin(s) > chip)
            def _():
                pl.semaphore_wait(ready.at[twin(s)], 1)

        to_twin(s).start()

    keep = pltpu.make_async_copy(rows_of(chip), rrecv.at[core, chip], bank_sem)
    keep.start()

    met = [order[0]] + [s for s in order if along[s] != along[order[0]]][:1]

    @pl.loop(chip + 1, chips)
    def _(q):
        fresh = functools.reduce(jnp.logical_and, [q != twin(s) for s in met])

        @pl.when(fresh)
        def _():
            pl.semaphore_wait(ready.at[q], 1)

        send_records(q).start()

    others = pl.ds(0, chips - 1)
    forward = push(rrecv.at[core], rrecv.at[core], fs_sem, fr_sem, partner)
    for s in order:
        if s == order[-1]:
            keep.wait()
            landed(rrecv.at[0, others], rr_sem)
            forward.start()
        landed(pair_in.at[s], pr_sem.at[s])
        theirs = lax.div(plan_ref[s], 2) == twin(s)
        for i in range(chips // 2):
            pair_out[s, i] = jnp.where(theirs, pair_in[s, i], tcomb[s, side(s, chip), i])

        @pl.loop(0, chips // 2)
        def _(i):
            @pl.when(i != place(s, chip))
            def _():
                spread(s, i).start()

    rows = steps * kk

    for s in range(steps):
        tpair[s][place(s, chip)] = pair_out[s, place(s, chip)]
    forward.wait_recv()

    for v in range(halves):
        for a in range(n):
            xs[v, a * own : (a + 1) * own, :] = rrecv[a % 2, a // 2, :, v * LANES : (v + 1) * LANES].astype(
                jnp.float32
            )
        xs[v, n * own :, :] = jnp.zeros((xs.shape[1] - n * own, LANES), jnp.float32)
    shift = lax.broadcasted_iota(jnp.int32, (part, width * LANES), 1) - lax.broadcasted_iota(
        jnp.int32, (part, width * LANES), 0
    )
    band = jnp.where((shift >= 0) & (shift < taps), 1.0, 0.0).astype(jnp.bfloat16)
    live = jnp.sum(mask_v[...].astype(jnp.float32), axis=1, keepdims=True)
    scale = jnp.sqrt(taps / (1.0 + live))
    left = lax.broadcasted_iota(jnp.int32, (n, LANES), 1) < part

    def frame(i, carry):
        tiles = [
            xs[q % halves, pl.ds(i + (q // halves) * own, n, stride=own), :] for q in range(halves + width)
        ]
        turned = [pltpu.roll(tile, part, 1) for tile in tiles]
        odd = [jnp.where(left, turned[q], turned[q + 1]) for q in range(halves + width - 1)]
        x = jnp.concatenate(
            [jnp.concatenate(some[h : h + width], axis=1) for some in (tiles, odd) for h in range(halves)], axis=0
        )
        frames[i] = x.astype(jnp.bfloat16)
        sq = x * x
        high = sq.astype(jnp.bfloat16)
        low = (sq - high.astype(jnp.float32)).astype(jnp.bfloat16)
        energy = lax.dot_general(
            jnp.concatenate([high, low], axis=0), band, dims, preferred_element_type=jnp.float32
        )
        energy = energy[: 2 * halves * n] + energy[2 * halves * n :]
        factor = scale * mask_s[chip * own + i].astype(jnp.float32)
        inv[i] = factor / jnp.sqrt(energy + 1e-06)
        return carry

    lax.fori_loop(0, own, frame, 0, unroll=own)

    for s in order:
        landed(tpair[s].at[pl.ds(0, chips // 2 - 1)], qr_sem.at[s])
        for j in range(kk):
            got = tpair[s][place(s, lax.div(plan_ref[s], 2)), j]
            got = got.astype(jnp.float32)
            tmpl[...] = jnp.concatenate([got, jnp.zeros((own, width * LANES - taps), jnp.float32)], axis=1)
            energy = jnp.sum(got * got, axis=1, keepdims=True)
            wts[...] = jnp.broadcast_to(1.0 / jnp.sqrt(energy + 1e-06), (own, part))

            def channel(i, total):
                base = jnp.broadcast_to(tmpl[pl.ds(i, 1), :], (16, width * LANES)).astype(jnp.bfloat16)
                base = jnp.concatenate([base] * (part // 16), axis=0)
                taps_of = pltpu.roll(base, 0, 1, stride=1, stride_axis=0)
                raw = lax.dot_general(frames[i], taps_of, dims, preferred_element_type=jnp.float32)
                return total + raw * inv[i] * wts[pl.ds(i, 1), :]

            total = lax.fori_loop(0, own, channel, jnp.zeros((2 * halves * n, part), jnp.float32), unroll=own)
            total = jnp.concatenate([total[: halves * n], total[halves * n :]], axis=1)
            at = (s * kk + j) * halves * n
            acc[at : at + halves * n, :] = total

    for d in range(n):
        for h in range(halves):
            osend[d, :, h * LANES : (h + 1) * LANES] = acc[pl.ds(h * n + d, rows, stride=halves * n), :]

    def give(d):
        return push(osend.at[d], out_ref.at[core * chips + chip], os_sem, or_sem, d)

    @pl.loop(0, me)
    def _(d):
        give(d).start()

    @pl.loop(me + 1, n)
    def _(d):
        give(d).start()

    mine = pltpu.make_async_copy(osend.at[me], out_ref.at[core * chips + chip], bank_sem)
    mine.start()
    sent(tsend, cs_sem)
    sent(pair_in, ps_sem)
    sent(pair_out.at[:, pl.ds(0, chips // 2 - 1)], qs_sem)
    sent(rrecv.at[0, others], rs_sem)
    forward.wait_send()
    sent(osend.at[pl.ds(0, n - 1)], os_sem)
    mine.wait()
    landed(out_ref.at[pl.ds(0, n - 1)], or_sem)


def shards(records, bank, plan, template_ids, channel_mask):
    n = lax.axis_size("tm")
    chips = n // 2
    steps, kcount = template_ids.shape
    chans, block = records.shape
    slots, _, taps = bank.shape
    kk = kcount // 2
    own = up(-(-chans // chips), 8)
    if own * chips != chans:
        more = own * chips - chans
        records = jnp.pad(records, ((0, more), (0, 0)))
        bank = jnp.pad(bank, ((0, 0), (0, more), (0, 0)))
        channel_mask = jnp.pad(channel_mask, (0, more))
    halves = block // LANES
    part = LANES // 2
    width = up(part + taps - 1, LANES) // LANES
    hbm = pl.BlockSpec(memory_space=pl.ANY)
    f32, bf16 = jnp.float32, jnp.bfloat16
    dma = pltpu.SemaphoreType.DMA
    extra = -(-(halves + width - 1) // halves)
    rows = steps * kk
    piece = (kk, own, taps)
    parts = pl.pallas_call(
        functools.partial(kernel, n, steps, kk, taps),
        out_shape=jax.ShapeDtypeStruct((n, rows, block), f32),
        in_specs=[hbm] * 6,
        out_specs=hbm,
        scratch_shapes=[
            pltpu.SMEM((steps,), jnp.int32),
            pltpu.SMEM((kcount, steps), jnp.int32),
            pltpu.SMEM(channel_mask.shape, jnp.int32),
            pltpu.VMEM((1, channel_mask.shape[0]), jnp.int32),
            pltpu.VMEM(bank.shape, bf16),
            pltpu.VMEM((steps, 2, chips // 2, *piece), bf16),
            pltpu.VMEM((steps, 2, chips // 2, *piece), bf16),
            pltpu.VMEM((steps, 2, chips // 2, *piece), bf16),
            pltpu.VMEM((steps, chips // 2, *piece), bf16),
            pltpu.VMEM((steps, chips // 2, *piece), bf16),
            [pltpu.VMEM((chips // 2, *piece), bf16)] * steps,
            pltpu.VMEM((2, chips, own, block), bf16),
            pltpu.VMEM((halves, (n + extra) * own, LANES), f32),
            pltpu.VMEM((own, 2 * halves * n, width * LANES), bf16),
            pltpu.VMEM((own, 2 * halves * n, part), f32),
            pltpu.VMEM((own, width * LANES), f32),
            pltpu.VMEM((own, part), f32),
            pltpu.VMEM((rows * halves * n, LANES), f32),
            pltpu.VMEM((n, rows, block), f32),
            pltpu.SemaphoreType.REGULAR((chips,)),
            dma((4,)), dma(()), dma(()), dma(()), dma(()), dma(()), dma(()), dma((steps,)), dma(()),
            dma((steps,)), dma(()), dma((steps,)), dma(()), dma(()),
        ],
        compiler_params=pltpu.CompilerParams(
            collective_id=0, has_side_effects=True, vmem_limit_bytes=60 * 1024 * 1024
        ),
        name="detect",
    )(plan, template_ids.T, channel_mask, channel_mask.reshape(1, -1), records, bank)
    sums = jnp.sum(parts.reshape(2, chips, steps, kk, block), axis=1)
    return jnp.swapaxes(sums, 0, 1).reshape(steps, kcount, block)


def solution(mesh):
    placed = (
        P("groups", "tm"),
        P("tm", "groups", None),
        P("groups"),
        P("groups", None),
        P("groups"),
    )
    return jax.shard_map(
        shards, mesh=mesh, in_specs=placed, out_specs=P("groups", None, "tm"), check_vma=False
    )
```

```python
import functools

import jax
import jax.numpy as jnp
from jax import lax
from jax.experimental import pallas as pl
from jax.experimental.pallas import tpu as pltpu
from jax.sharding import PartitionSpec as P

MESH = pl.DeviceIdType.MESH
LANES = 128
ALONG = (1, 0, 0)
ORDER = (0, 1, 2)


def up(value, unit):
    return -(-value // unit) * unit


def kernel(
    n, steps, kk, taps,
    plan_in, ids_in, mask_in, row_in, rec_ref, bank_ref, out_ref,
    plan_ref, ids_ref, mask_s, mask_v, bank_v, tsend, tpart, tcomb, pair_in, pair_out, tpair, rrecv,
    xs, frames, inv, tmpl, wts, acc, osend,
    ready, few_sem, bank_sem, rs_sem, rr_sem, fs_sem, fr_sem, cs_sem, cr_sem, ps_sem, pr_sem,
    qs_sem, qr_sem, os_sem, or_sem,
):
    me = lax.axis_index("tm")
    chip, core = me // 2, me % 2
    chips = n // 2
    partner = me + 1 - 2 * core
    chans, block = rec_ref.shape
    own = chans // chips
    halves = block // LANES
    part = LANES // 2
    width = frames.shape[2] // LANES
    dims = (((1,), (1,)), ((), ()))
    along = [ALONG[s % len(ALONG)] for s in range(steps)]
    order = sorted(range(steps), key=lambda s: ORDER[s % len(ORDER)])

    def side(s, q):
        return q // (1 + along[s]) % 2

    def place(s, q):
        return q // 4 * 2 + q % 2 if along[s] else q // 2

    def chip_at(s, i):
        return i // 2 * 4 + side(s, chip) * 2 + i % 2 if along[s] else i * 2 + side(s, chip)

    def twin(s):
        return chip + (1 - 2 * side(s, chip)) * (1 + along[s])


    def tell(sem, to):
        pl.semaphore_signal(sem, inc=1, device_id={"tm": to}, device_id_type=MESH)

    def push(src, dst, send_sem, recv_sem, to):
        return pltpu.make_async_remote_copy(
            src_ref=src, dst_ref=dst, send_sem=send_sem, recv_sem=recv_sem,
            device_id={"tm": to}, device_id_type=MESH,
        )

    def sent(ref, sem):
        push(ref, ref, sem, sem, partner).wait_send()

    def landed(ref, sem):
        push(ref, ref, sem, sem, partner).wait_recv()

    fetch = pltpu.make_async_copy(bank_ref, bank_v, bank_sem)
    fetch.start()
    few = [
        pltpu.make_async_copy(src, dst, few_sem.at[i])
        for i, (src, dst) in enumerate([(plan_in, plan_ref), (ids_in, ids_ref), (mask_in, mask_s), (row_in, mask_v)])
    ]
    for copy in few:
        copy.start()
    barrier = pltpu.get_barrier_semaphore()
    tell(barrier, partner)

    @pl.loop(chip + 1, chips)
    def _(q):
        tell(barrier, 2 * q + core)

    pl.semaphore_wait(barrier, 1 + chip)
    def rows_of(q):
        return rec_ref.at[pl.ds(pl.multiple_of(q * own, 8), own)]

    def send_records(q):
        return push(rows_of(q), rrecv.at[core, chip], rs_sem, rr_sem, 2 * q + core)

    def across(s):
        return push(tsend.at[s], tpart.at[s], cs_sem, cr_sem.at[s], partner)

    def to_twin(s):
        return push(tcomb.at[s, 1 - side(s, chip)], pair_in.at[s], ps_sem, pr_sem.at[s], 2 * twin(s) + core)

    def spread(s, i):
        return push(
            pair_out.at[s, i], tpair[s].at[place(s, chip)], qs_sem, qr_sem.at[s], 2 * chip_at(s, i) + core
        )

    @pl.loop(0, chip)
    def _(q):
        tell(ready.at[chip], 2 * q + core)

    for copy in few:
        copy.wait()
    fetch.wait()
    for s in order:
        for j in range(kk):
            pick = bank_v[ids_ref[(1 - core) * kk + j, s]]
            for q in range(chips):
                tsend[s, side(s, q), place(s, q), j] = pick[q * own : (q + 1) * own]
        across(s).start()

    @pl.loop(0, chip)
    def _(q):
        send_records(q).start()

    for s in order:
        theirs = plan_ref[s] == partner
        across(s).wait_recv()
        for j in range(kk):
            pick = bank_v[ids_ref[core * kk + j, s]]
            for q in range(chips):
                at = (s, side(s, q), place(s, q), j)
                tcomb[at] = jnp.where(theirs, tpart[at], pick[q * own : (q + 1) * own])
        if s == min(order, key=lambda t: (along[t] != along[s], order.index(t))):

            @pl.when(twin(s) > chip)
            def _():
                pl.semaphore_wait(ready.at[twin(s)], 1)

        to_twin(s).start()

    keep = pltpu.make_async_copy(rows_of(chip), rrecv.at[core, chip], bank_sem)
    keep.start()

    met = [order[0]] + [s for s in order if along[s] != along[order[0]]][:1]

    @pl.loop(chip + 1, chips)
    def _(q):
        fresh = functools.reduce(jnp.logical_and, [q != twin(s) for s in met])

        @pl.when(fresh)
        def _():
            pl.semaphore_wait(ready.at[q], 1)

        send_records(q).start()

    others = pl.ds(0, chips - 1)
    forward = push(rrecv.at[core], rrecv.at[core], fs_sem, fr_sem, partner)
    for s in order:
        if s == order[-1]:
            keep.wait()
            landed(rrecv.at[0, others], rr_sem)
            forward.start()
        landed(pair_in.at[s], pr_sem.at[s])
        theirs = lax.div(plan_ref[s], 2) == twin(s)
        for i in range(chips // 2):
            pair_out[s, i] = jnp.where(theirs, pair_in[s, i], tcomb[s, side(s, chip), i])

        @pl.loop(0, chips // 2)
        def _(i):
            @pl.when(i != place(s, chip))
            def _():
                spread(s, i).start()

    rows = steps * kk

    for s in range(steps):
        tpair[s][place(s, chip)] = pair_out[s, place(s, chip)]
    forward.wait_recv()

    for v in range(halves):
        for a in range(n):
            xs[v, a * own : (a + 1) * own, :] = rrecv[a % 2, a // 2, :, v * LANES : (v + 1) * LANES].astype(
                jnp.float32
            )
        xs[v, n * own :, :] = jnp.zeros((xs.shape[1] - n * own, LANES), jnp.float32)
    shift = lax.broadcasted_iota(jnp.int32, (part, width * LANES), 1) - lax.broadcasted_iota(
        jnp.int32, (part, width * LANES), 0
    )
    band = jnp.where((shift >= 0) & (shift < taps), 1.0, 0.0).astype(jnp.bfloat16)
    live = jnp.sum(mask_v[...].astype(jnp.float32), axis=1, keepdims=True)
    scale = jnp.sqrt(taps / (1.0 + live))
    left = lax.broadcasted_iota(jnp.int32, (n, LANES), 1) < part

    def frame(i, carry):
        tiles = [
            xs[q % halves, pl.ds(i + (q // halves) * own, n, stride=own), :] for q in range(halves + width)
        ]
        turned = [pltpu.roll(tile, part, 1) for tile in tiles]
        odd = [jnp.where(left, turned[q], turned[q + 1]) for q in range(halves + width - 1)]
        x = jnp.concatenate(
            [jnp.concatenate(some[h : h + width], axis=1) for some in (tiles, odd) for h in range(halves)], axis=0
        )
        frames[i] = x.astype(jnp.bfloat16)
        sq = x * x
        high = sq.astype(jnp.bfloat16)
        low = (sq - high.astype(jnp.float32)).astype(jnp.bfloat16)
        energy = lax.dot_general(
            jnp.concatenate([high, low], axis=0), band, dims, preferred_element_type=jnp.float32
        )
        energy = energy[: 2 * halves * n] + energy[2 * halves * n :]
        factor = scale * mask_s[chip * own + i].astype(jnp.float32)
        inv[i] = factor / jnp.sqrt(energy + 1e-06)
        return carry

    lax.fori_loop(0, own, frame, 0, unroll=own)

    for group in [[s] for s in order]:
        turns = [(s, j) for s in group for j in range(kk)]
        for s, j in turns:
            if j == 0:
                landed(tpair[s].at[pl.ds(0, chips // 2 - 1)], qr_sem.at[s])
            r = s * kk + j
            got = tpair[s][place(s, lax.div(plan_ref[s], 2)), j].astype(jnp.float32)
            tmpl[r] = jnp.concatenate([got, jnp.zeros((own, width * LANES - taps), jnp.float32)], axis=1)
            energy = jnp.sum(got * got, axis=1, keepdims=True)
            wts[r] = jnp.broadcast_to(1.0 / jnp.sqrt(energy + 1e-06), (own, part))

        def channel(i, totals):
            sums = []
            for (s, j), total in zip(turns, totals):
                r = s * kk + j
                base = jnp.broadcast_to(tmpl[r, pl.ds(i, 1), :], (16, width * LANES)).astype(jnp.bfloat16)
                base = jnp.concatenate([base] * (part // 16), axis=0)
                taps_of = pltpu.roll(base, 0, 1, stride=1, stride_axis=0)
                raw = lax.dot_general(frames[i], taps_of, dims, preferred_element_type=jnp.float32)
                sums.append(total + raw * inv[i] * wts[r, pl.ds(i, 1), :])
            return tuple(sums)

        none = jnp.zeros((2 * halves * n, part), jnp.float32)
        totals = lax.fori_loop(0, own, channel, (none,) * len(turns), unroll=own)
        for (s, j), total in zip(turns, totals):
            total = jnp.concatenate([total[: halves * n], total[halves * n :]], axis=1)
            at = (s * kk + j) * halves * n
            acc[at : at + halves * n, :] = total

    for d in range(n):
        for h in range(halves):
            osend[d, :, h * LANES : (h + 1) * LANES] = acc[pl.ds(h * n + d, rows, stride=halves * n), :]

    def give(d):
        return push(osend.at[d], out_ref.at[core * chips + chip], os_sem, or_sem, d)

    @pl.loop(0, me)
    def _(d):
        give(d).start()

    @pl.loop(me + 1, n)
    def _(d):
        give(d).start()

    mine = pltpu.make_async_copy(osend.at[me], out_ref.at[core * chips + chip], bank_sem)
    mine.start()
    sent(tsend, cs_sem)
    sent(pair_in, ps_sem)
    sent(pair_out.at[:, pl.ds(0, chips // 2 - 1)], qs_sem)
    sent(rrecv.at[0, others], rs_sem)
    forward.wait_send()
    sent(osend.at[pl.ds(0, n - 1)], os_sem)
    mine.wait()
    landed(out_ref.at[pl.ds(0, n - 1)], or_sem)


def shards(records, bank, plan, template_ids, channel_mask):
    n = lax.axis_size("tm")
    chips = n // 2
    steps, kcount = template_ids.shape
    chans, block = records.shape
    slots, _, taps = bank.shape
    kk = kcount // 2
    own = up(-(-chans // chips), 8)
    if own * chips != chans:
        more = own * chips - chans
        records = jnp.pad(records, ((0, more), (0, 0)))
        bank = jnp.pad(bank, ((0, 0), (0, more), (0, 0)))
        channel_mask = jnp.pad(channel_mask, (0, more))
    halves = block // LANES
    part = LANES // 2
    width = up(part + taps - 1, LANES) // LANES
    hbm = pl.BlockSpec(memory_space=pl.ANY)
    f32, bf16 = jnp.float32, jnp.bfloat16
    dma = pltpu.SemaphoreType.DMA
    extra = -(-(halves + width - 1) // halves)
    rows = steps * kk
    piece = (kk, own, taps)
    parts = pl.pallas_call(
        functools.partial(kernel, n, steps, kk, taps),
        out_shape=jax.ShapeDtypeStruct((n, rows, block), f32),
        in_specs=[hbm] * 6,
        out_specs=hbm,
        scratch_shapes=[
            pltpu.SMEM((steps,), jnp.int32),
            pltpu.SMEM((kcount, steps), jnp.int32),
            pltpu.SMEM(channel_mask.shape, jnp.int32),
            pltpu.VMEM((1, channel_mask.shape[0]), jnp.int32),
            pltpu.VMEM(bank.shape, bf16),
            pltpu.VMEM((steps, 2, chips // 2, *piece), bf16),
            pltpu.VMEM((steps, 2, chips // 2, *piece), bf16),
            pltpu.VMEM((steps, 2, chips // 2, *piece), bf16),
            pltpu.VMEM((steps, chips // 2, *piece), bf16),
            pltpu.VMEM((steps, chips // 2, *piece), bf16),
            [pltpu.VMEM((chips // 2, *piece), bf16)] * steps,
            pltpu.VMEM((2, chips, own, block), bf16),
            pltpu.VMEM((halves, (n + extra) * own, LANES), f32),
            pltpu.VMEM((own, 2 * halves * n, width * LANES), bf16),
            pltpu.VMEM((own, 2 * halves * n, part), f32),
            pltpu.VMEM((steps * kk, own, width * LANES), f32),
            pltpu.VMEM((steps * kk, own, part), f32),
            pltpu.VMEM((rows * halves * n, LANES), f32),
            pltpu.VMEM((n, rows, block), f32),
            pltpu.SemaphoreType.REGULAR((chips,)),
            dma((4,)), dma(()), dma(()), dma(()), dma(()), dma(()), dma(()), dma((steps,)), dma(()),
            dma((steps,)), dma(()), dma((steps,)), dma(()), dma(()),
        ],
        compiler_params=pltpu.CompilerParams(
            collective_id=0, has_side_effects=True, vmem_limit_bytes=60 * 1024 * 1024
        ),
        name="detect",
    )(plan, template_ids.T, channel_mask, channel_mask.reshape(1, -1), records, bank)
    sums = jnp.sum(parts.reshape(2, chips, steps, kk, block), axis=1)
    return jnp.swapaxes(sums, 0, 1).reshape(steps, kcount, block)


def solution(mesh):
    placed = (
        P("groups", "tm"),
        P("tm", "groups", None),
        P("groups"),
        P("groups", None),
        P("groups"),
    )
    return jax.shard_map(
        shards, mesh=mesh, in_specs=placed, out_specs=P("groups", None, "tm"), check_vma=False
    )
```

```python
import functools

import jax
import jax.numpy as jnp
from jax import lax
from jax.experimental import pallas as pl
from jax.experimental.pallas import tpu as pltpu
from jax.sharding import PartitionSpec as P

MESH = pl.DeviceIdType.MESH
LANES = 128
ALONG = (1, 0, 0)
ORDER = (0, 1, 2)


def up(value, unit):
    return -(-value // unit) * unit


def kernel(
    n, steps, kk, taps,
    plan_in, ids_in, mask_in, row_in, rec_ref, bank_ref, out_ref,
    plan_ref, ids_ref, mask_s, mask_v, bank_v, tsend, tpart, tcomb, pair_in, pair_out, tpair, rrecv,
    xs, frames, inv, tmpl, wts, acc, osend,
    ready, few_sem, bank_sem, rs_sem, rr_sem, fs_sem, fr_sem, cs_sem, cr_sem, ps_sem, pr_sem,
    qs_sem, qr_sem, os_sem, or_sem,
):
    me = lax.axis_index("tm")
    chip, core = me // 2, me % 2
    chips = n // 2
    partner = me + 1 - 2 * core
    chans, block = rec_ref.shape
    own = chans // chips
    halves = block // LANES
    part = LANES // 2
    width = frames.shape[2] // LANES
    dims = (((1,), (1,)), ((), ()))
    along = [ALONG[s % len(ALONG)] for s in range(steps)]
    order = sorted(range(steps), key=lambda s: ORDER[s % len(ORDER)])

    def side(s, q):
        return q // (1 + along[s]) % 2

    def place(s, q):
        return q // 4 * 2 + q % 2 if along[s] else q // 2

    def chip_at(s, i):
        return i // 2 * 4 + side(s, chip) * 2 + i % 2 if along[s] else i * 2 + side(s, chip)

    def twin(s):
        return chip + (1 - 2 * side(s, chip)) * (1 + along[s])


    def tell(sem, to):
        pl.semaphore_signal(sem, inc=1, device_id={"tm": to}, device_id_type=MESH)

    def push(src, dst, send_sem, recv_sem, to):
        return pltpu.make_async_remote_copy(
            src_ref=src, dst_ref=dst, send_sem=send_sem, recv_sem=recv_sem,
            device_id={"tm": to}, device_id_type=MESH,
        )

    def sent(ref, sem):
        push(ref, ref, sem, sem, partner).wait_send()

    def landed(ref, sem):
        push(ref, ref, sem, sem, partner).wait_recv()

    barrier = pltpu.get_barrier_semaphore()
    tell(barrier, partner)

    @pl.loop(chip + 1, chips)
    def _(q):
        tell(barrier, 2 * q + core)

    fetch = pltpu.make_async_copy(bank_ref, bank_v, bank_sem)
    fetch.start()
    few = [
        pltpu.make_async_copy(src, dst, few_sem.at[i])
        for i, (src, dst) in enumerate([(plan_in, plan_ref), (ids_in, ids_ref), (mask_in, mask_s), (row_in, mask_v)])
    ]
    for copy in few:
        copy.start()
    pl.semaphore_wait(barrier, 1 + chip)
    def rows_of(q):
        return rec_ref.at[pl.ds(pl.multiple_of(q * own, 8), own)]

    def send_records(q):
        return push(rows_of(q), rrecv.at[core, chip], rs_sem, rr_sem, 2 * q + core)

    def across(s):
        return push(tsend.at[s], tpart.at[s], cs_sem, cr_sem.at[s], partner)

    def to_twin(s):
        return push(tcomb.at[s, 1 - side(s, chip)], pair_in.at[s], ps_sem, pr_sem.at[s], 2 * twin(s) + core)

    def spread(s, i):
        return push(
            pair_out.at[s, i], tpair[s].at[place(s, chip)], qs_sem, qr_sem.at[s], 2 * chip_at(s, i) + core
        )

    @pl.loop(0, chip)
    def _(q):
        tell(ready.at[chip], 2 * q + core)

    for copy in few:
        copy.wait()
    fetch.wait()
    for s in order:
        for j in range(kk):
            pick = bank_v[ids_ref[(1 - core) * kk + j, s]]
            for q in range(chips):
                tsend[s, side(s, q), place(s, q), j] = pick[q * own : (q + 1) * own]
        across(s).start()

    @pl.loop(0, chip)
    def _(q):
        send_records(q).start()

    for s in order:
        theirs = plan_ref[s] == partner
        across(s).wait_recv()
        for j in range(kk):
            pick = bank_v[ids_ref[core * kk + j, s]]
            for q in range(chips):
                at = (s, side(s, q), place(s, q), j)
                tcomb[at] = jnp.where(theirs, tpart[at], pick[q * own : (q + 1) * own])
        if s == min(order, key=lambda t: (along[t] != along[s], order.index(t))):

            @pl.when(twin(s) > chip)
            def _():
                pl.semaphore_wait(ready.at[twin(s)], 1)

        to_twin(s).start()

    keep = pltpu.make_async_copy(rows_of(chip), rrecv.at[core, chip], bank_sem)
    keep.start()

    met = [order[0]] + [s for s in order if along[s] != along[order[0]]][:1]

    @pl.loop(chip + 1, chips)
    def _(q):
        fresh = functools.reduce(jnp.logical_and, [q != twin(s) for s in met])

        @pl.when(fresh)
        def _():
            pl.semaphore_wait(ready.at[q], 1)

        send_records(q).start()

    others = pl.ds(0, chips - 1)
    forward = push(rrecv.at[core], rrecv.at[core], fs_sem, fr_sem, partner)
    for s in order:
        if s == order[-1]:
            keep.wait()
            landed(rrecv.at[0, others], rr_sem)
            forward.start()
        landed(pair_in.at[s], pr_sem.at[s])
        theirs = lax.div(plan_ref[s], 2) == twin(s)
        for i in range(chips // 2):
            pair_out[s, i] = jnp.where(theirs, pair_in[s, i], tcomb[s, side(s, chip), i])

        @pl.loop(0, chips // 2)
        def _(i):
            @pl.when(i != place(s, chip))
            def _():
                spread(s, i).start()

    rows = steps * kk

    for s in range(steps):
        tpair[s][place(s, chip)] = pair_out[s, place(s, chip)]
    forward.wait_recv()

    for v in range(halves):
        for a in range(n):
            xs[v, a * own : (a + 1) * own, :] = rrecv[a % 2, a // 2, :, v * LANES : (v + 1) * LANES].astype(
                jnp.float32
            )
        xs[v, n * own :, :] = jnp.zeros((xs.shape[1] - n * own, LANES), jnp.float32)
    shift = lax.broadcasted_iota(jnp.int32, (part, width * LANES), 1) - lax.broadcasted_iota(
        jnp.int32, (part, width * LANES), 0
    )
    band = jnp.where((shift >= 0) & (shift < taps), 1.0, 0.0).astype(jnp.bfloat16)
    live = jnp.sum(mask_v[...].astype(jnp.float32), axis=1, keepdims=True)
    scale = jnp.sqrt(taps / (1.0 + live))
    left = lax.broadcasted_iota(jnp.int32, (n, LANES), 1) < part

    def frame(i, carry):
        tiles = [
            xs[q % halves, pl.ds(i + (q // halves) * own, n, stride=own), :] for q in range(halves + width)
        ]
        turned = [pltpu.roll(tile, part, 1) for tile in tiles]
        odd = [jnp.where(left, turned[q], turned[q + 1]) for q in range(halves + width - 1)]
        x = jnp.concatenate(
            [jnp.concatenate(some[h : h + width], axis=1) for some in (tiles, odd) for h in range(halves)], axis=0
        )
        frames[i] = x.astype(jnp.bfloat16)
        sq = x * x
        high = sq.astype(jnp.bfloat16)
        low = (sq - high.astype(jnp.float32)).astype(jnp.bfloat16)
        energy = lax.dot_general(
            jnp.concatenate([high, low], axis=0), band, dims, preferred_element_type=jnp.float32
        )
        energy = energy[: 2 * halves * n] + energy[2 * halves * n :]
        factor = scale * mask_s[chip * own + i].astype(jnp.float32)
        inv[i] = factor / jnp.sqrt(energy + 1e-06)
        return carry

    lax.fori_loop(0, own, frame, 0, unroll=own)

    for group in [[s] for s in order]:
        turns = [(s, j) for s in group for j in range(kk)]
        for s, j in turns:
            if j == 0:
                landed(tpair[s].at[pl.ds(0, chips // 2 - 1)], qr_sem.at[s])
            r = s * kk + j
            got = tpair[s][place(s, lax.div(plan_ref[s], 2)), j].astype(jnp.float32)
            tmpl[r] = jnp.concatenate([got, jnp.zeros((own, width * LANES - taps), jnp.float32)], axis=1)
            energy = jnp.sum(got * got, axis=1, keepdims=True)
            wts[r] = jnp.broadcast_to(1.0 / jnp.sqrt(energy + 1e-06), (own, part))

        def channel(i, totals):
            sums = []
            for (s, j), total in zip(turns, totals):
                r = s * kk + j
                base = jnp.broadcast_to(tmpl[r, pl.ds(i, 1), :], (16, width * LANES)).astype(jnp.bfloat16)
                base = jnp.concatenate([base] * (part // 16), axis=0)
                taps_of = pltpu.roll(base, 0, 1, stride=1, stride_axis=0)
                raw = lax.dot_general(frames[i], taps_of, dims, preferred_element_type=jnp.float32)
                sums.append(total + raw * inv[i] * wts[r, pl.ds(i, 1), :])
            return tuple(sums)

        none = jnp.zeros((2 * halves * n, part), jnp.float32)
        totals = lax.fori_loop(0, own, channel, (none,) * len(turns), unroll=own)
        for (s, j), total in zip(turns, totals):
            total = jnp.concatenate([total[: halves * n], total[halves * n :]], axis=1)
            at = (s * kk + j) * halves * n
            acc[at : at + halves * n, :] = total

    for d in range(n):
        for h in range(halves):
            osend[d, :, h * LANES : (h + 1) * LANES] = acc[pl.ds(h * n + d, rows, stride=halves * n), :]

    def give(d):
        return push(osend.at[d], out_ref.at[core * chips + chip], os_sem, or_sem, d)

    @pl.loop(0, me)
    def _(d):
        give(d).start()

    @pl.loop(me + 1, n)
    def _(d):
        give(d).start()

    mine = pltpu.make_async_copy(osend.at[me], out_ref.at[core * chips + chip], bank_sem)
    mine.start()
    sent(tsend, cs_sem)
    sent(pair_in, ps_sem)
    sent(pair_out.at[:, pl.ds(0, chips // 2 - 1)], qs_sem)
    sent(rrecv.at[0, others], rs_sem)
    forward.wait_send()
    sent(osend.at[pl.ds(0, n - 1)], os_sem)
    mine.wait()
    landed(out_ref.at[pl.ds(0, n - 1)], or_sem)


def shards(records, bank, plan, template_ids, channel_mask):
    n = lax.axis_size("tm")
    chips = n // 2
    steps, kcount = template_ids.shape
    chans, block = records.shape
    slots, _, taps = bank.shape
    kk = kcount // 2
    own = up(-(-chans // chips), 8)
    if own * chips != chans:
        more = own * chips - chans
        records = jnp.pad(records, ((0, more), (0, 0)))
        bank = jnp.pad(bank, ((0, 0), (0, more), (0, 0)))
        channel_mask = jnp.pad(channel_mask, (0, more))
    halves = block // LANES
    part = LANES // 2
    width = up(part + taps - 1, LANES) // LANES
    hbm = pl.BlockSpec(memory_space=pl.ANY)
    f32, bf16 = jnp.float32, jnp.bfloat16
    dma = pltpu.SemaphoreType.DMA
    extra = -(-(halves + width - 1) // halves)
    rows = steps * kk
    piece = (kk, own, taps)
    parts = pl.pallas_call(
        functools.partial(kernel, n, steps, kk, taps),
        out_shape=jax.ShapeDtypeStruct((n, rows, block), f32),
        in_specs=[hbm] * 6,
        out_specs=hbm,
        scratch_shapes=[
            pltpu.SMEM((steps,), jnp.int32),
            pltpu.SMEM((kcount, steps), jnp.int32),
            pltpu.SMEM(channel_mask.shape, jnp.int32),
            pltpu.VMEM((1, channel_mask.shape[0]), jnp.int32),
            pltpu.VMEM(bank.shape, bf16),
            pltpu.VMEM((steps, 2, chips // 2, *piece), bf16),
            pltpu.VMEM((steps, 2, chips // 2, *piece), bf16),
            pltpu.VMEM((steps, 2, chips // 2, *piece), bf16),
            pltpu.VMEM((steps, chips // 2, *piece), bf16),
            pltpu.VMEM((steps, chips // 2, *piece), bf16),
            [pltpu.VMEM((chips // 2, *piece), bf16)] * steps,
            pltpu.VMEM((2, chips, own, block), bf16),
            pltpu.VMEM((halves, (n + extra) * own, LANES), f32),
            pltpu.VMEM((own, 2 * halves * n, width * LANES), bf16),
            pltpu.VMEM((own, 2 * halves * n, part), f32),
            pltpu.VMEM((steps * kk, own, width * LANES), f32),
            pltpu.VMEM((steps * kk, own, part), f32),
            pltpu.VMEM((rows * halves * n, LANES), f32),
            pltpu.VMEM((n, rows, block), f32),
            pltpu.SemaphoreType.REGULAR((chips,)),
            dma((4,)), dma(()), dma(()), dma(()), dma(()), dma(()), dma(()), dma((steps,)), dma(()),
            dma((steps,)), dma(()), dma((steps,)), dma(()), dma(()),
        ],
        compiler_params=pltpu.CompilerParams(
            collective_id=0, has_side_effects=True, vmem_limit_bytes=60 * 1024 * 1024
        ),
        name="detect",
    )(plan, template_ids.T, channel_mask, channel_mask.reshape(1, -1), records, bank)
    sums = jnp.sum(parts.reshape(2, chips, steps, kk, block), axis=1)
    return jnp.swapaxes(sums, 0, 1).reshape(steps, kcount, block)


def solution(mesh):
    placed = (
        P("groups", "tm"),
        P("tm", "groups", None),
        P("groups"),
        P("groups", None),
        P("groups"),
    )
    return jax.shard_map(
        shards, mesh=mesh, in_specs=placed, out_specs=P("groups", None, "tm"), check_vma=False
    )
```
